512 devices in a mesh: req: 64 (over x, y, core), head: 8 (over z).
Axes of the slice: x: 4, y: 8, z: 8, core: 2. Of those that a mesh axis runs over, the one named last changes fastest.
Arguments:
- hidden: bfloat16 [512, 4096], P(None, 'req'), may hold values from -16 to 16
- query_key_value_weight: bfloat16 [4096, 8, 768], P('req', 'head'), may hold values from -0.1875 to 0.1875
- output_weight: bfloat16 [4096, 4096], P('head', 'req'), may hold values from -0.375 to 0.375
- kv_pool: bfloat16 [4096, 8, 128, 256], P('req', 'head'), may hold values from -68 to 68
- lengths: int32 [512], P('req'), may hold values from 513 to 2048, as said below
- page_table: int32 [512, 16], P('req'), may hold values from 0 to 127, as said below
- send_slots: int32 [4096], P('req'), may hold values from 0 to 63, as said below
Outputs:
- attn_out: bfloat16 [512, 4096], P('head', 'req')
The draws below stay inside these ranges and needn't reach their ends.
Inputs may be any that keep to these rules, and one draw needn't show every extreme that they name: `page_table`: A request's live positions name distinct slots of its group's store, and every other entry is 0. Slots below 64 are the group's own pool rows; slot 64 + s is the page that group s sends to it. Every group uses exactly 32 of the 64 pages sent to it, never for a long request. `send_slots`: every group sends one page to every group; rows whose page the receiver does not use name an arbitrary slot. In 16 of the groups one request is long (more than (15) * 128 tokens); all others hold at most 768 tokens. The new token sits at position lengths[r].
All inputs are finite; a program needn't handle non-finite values.
Results may differ from the reference program's by a relative error of at most 0.018.
Values may be sent and summed in bfloat16 or wider, within the bound.
A program may use at most 64 MiB of HBM per device.

```python
import jax
import jax.numpy as jnp
from jax import lax

MODEL_WIDTH = 4096
KEY_HEADS = 8
QUERY_PER_KEY = 4
HEAD_SIZE = 128
PAGE_TOKENS = 128
SHORTP = 6
LONG_PAGES = 16
GROUP_REQUESTS = 8
REQUEST_GROUPS = 64
TOTAL_REQUESTS = 512
POOL_PAGES = 64


def plan(key):
    base_key = jax.random.fold_in(key, 4242)
    long_order = jax.random.permutation(jax.random.fold_in(base_key, 1), REQUEST_GROUPS)
    offset_values = jnp.arange(REQUEST_GROUPS, dtype=jnp.int32)
    offset_scores = jax.random.permutation(jax.random.fold_in(base_key, 2), REQUEST_GROUPS).astype(jnp.int32)
    offset_scores = offset_scores - jnp.where((offset_values == 1) | (offset_values == REQUEST_GROUPS // 2), 2 * REQUEST_GROUPS, 0)
    offset_scores = offset_scores - jnp.where(offset_values == REQUEST_GROUPS - 1, REQUEST_GROUPS, 0)
    offsets = jnp.argsort(offset_scores)[:REQUEST_GROUPS // 2].astype(jnp.int32)
    long_rank = jnp.argsort(long_order)

    def home(group_index):
        own_key = jax.random.fold_in(base_key, 1000 + group_index)
        short_len = jax.random.randint(jax.random.fold_in(own_key, 1), (GROUP_REQUESTS,), (SHORTP - 2) * PAGE_TOKENS + 1, SHORTP * PAGE_TOKENS + 1)
        longer = jax.random.randint(jax.random.fold_in(own_key, 2), (), (LONG_PAGES - 1) * PAGE_TOKENS + 1, LONG_PAGES * PAGE_TOKENS + 1)
        longer = jnp.where(long_rank[group_index] == 0, LONG_PAGES * PAGE_TOKENS, longer)
        long_spot = jax.random.randint(jax.random.fold_in(own_key, 3), (), 0, GROUP_REQUESTS)
        is_long = (jnp.arange(GROUP_REQUESTS) == long_spot) & (long_rank[group_index] < REQUEST_GROUPS // 4)
        group_lengths = jnp.where(is_long, longer, short_len)
        places = jnp.arange(LONG_PAGES)
        is_live = places[None, :] * PAGE_TOKENS < group_lengths[:, None]
        movable = (is_live & ~is_long[:, None]).reshape(-1)
        scores = jax.random.permutation(jax.random.fold_in(own_key, 4), GROUP_REQUESTS * LONG_PAGES) + jnp.where(movable, 0, GROUP_REQUESTS * LONG_PAGES)
        picked = jnp.argsort(scores)[:REQUEST_GROUPS // 2]
        sources = (group_index - offsets) % REQUEST_GROUPS
        remote = jnp.zeros((GROUP_REQUESTS * LONG_PAGES,), jnp.bool_).at[picked].set(True)
        remote_src = jnp.zeros((GROUP_REQUESTS * LONG_PAGES,), jnp.int32).at[picked].set(sources.astype(jnp.int32))
        is_local = is_live.reshape(-1) & ~remote
        rank_local = jnp.cumsum(is_local.astype(jnp.int32)) - 1
        pool_order = jax.random.permutation(jax.random.fold_in(own_key, 5), POOL_PAGES)
        local_slot = pool_order[jnp.clip(REQUEST_GROUPS // 2 + rank_local, 0, POOL_PAGES - 1)]
        group_table = jnp.where(remote, POOL_PAGES + remote_src, jnp.where(is_local, local_slot, 0))
        return (group_lengths.astype(jnp.int32), group_table.reshape(GROUP_REQUESTS, LONG_PAGES).astype(jnp.int32))

    def source(group_index):
        own_key = jax.random.fold_in(base_key, 1000 + group_index)
        pool_order = jax.random.permutation(jax.random.fold_in(own_key, 5), POOL_PAGES)
        filler = jax.random.randint(jax.random.fold_in(own_key, 6), (REQUEST_GROUPS,), 0, POOL_PAGES)
        targets = (group_index + offsets) % REQUEST_GROUPS
        return filler.at[targets].set(pool_order[:REQUEST_GROUPS // 2]).astype(jnp.int32)
    all_lengths, all_tables = jax.vmap(home)(jnp.arange(REQUEST_GROUPS))
    all_sends = jax.vmap(source)(jnp.arange(REQUEST_GROUPS))
    return (all_lengths.reshape(-1), all_tables.reshape(-1, LONG_PAGES), all_sends.reshape(-1))


def draw_lengths(key, part):
    return plan(key)[0]


def draw_page_table(key, part):
    return plan(key)[1]


def draw_send_slots(key, part):
    return plan(key)[2]


def draw_kv_pool(key, part):
    shape_of_pool = (REQUEST_GROUPS * POOL_PAGES, KEY_HEADS, PAGE_TOKENS, 2 * HEAD_SIZE)
    values = jnp.clip(jax.random.normal(jax.random.fold_in(key, 1), shape_of_pool, jnp.float32), -4.0, 4.0)
    return values.astype(jnp.bfloat16)


def raised(array, key, source, target, parts, factor):
    owner, partner = [(jnp.arange(array.shape[axis_at]) // (array.shape[axis_at] // parts)).reshape([-1 if axis == axis_at else 1 for axis in range(array.ndim)]) for axis_at in (source, target)]
    chosen = jax.random.permutation(key, parts)[partner]
    strong = (owner == chosen) | (owner == (partner + parts // 2) % parts)
    return jnp.where(strong, factor * array, array)


def levels(stream_key, extent, split, least, top_value):
    def one(position, parts):
        draws = jax.random.uniform(jax.random.fold_in(jax.random.fold_in(stream_key, 6), position), (parts,), jnp.float32, least / len(split), top_value / len(split))
        return jnp.repeat(jnp.exp(draws), extent[position] // parts).reshape((-1,) + (1,) * (len(extent) - position - 1))

    loudness = one(*split[0])
    for cut in split[1:]:
        loudness = loudness * one(*cut)
    return loudness


def bell_draw(rng, shape, scale, reach, cuts=(), kind=jnp.bfloat16):
    values = scale * jax.random.normal(rng, shape, jnp.float32)
    if cuts:
        values = values * levels(rng, shape, cuts, -0.22, 0.18)
    return jnp.clip(values, -reach, reach).astype(kind)


def gaussian_with(stream_key, extent, spread, limit, cuts, heavy, kind=jnp.bfloat16):
    array = spread * jax.random.normal(stream_key, extent, jnp.float32)
    if cuts:
        array = array * levels(stream_key, extent, cuts, -0.22, 0.18)
    return jnp.clip(raised(array, jax.random.fold_in(stream_key, 3), *heavy), -limit, limit).astype(kind)


def setup_inputs(seed: int = 0) -> dict:
    key_of = jax.random.split(jax.random.key(seed), 8)
    hidden = gaussian_with(key_of[0], (TOTAL_REQUESTS, MODEL_WIDTH), 1.0, 16.0, ((1, 64),), (1, 0, 64, 4.0))
    query_key_value_weight = bell_draw(key_of[1], (MODEL_WIDTH, KEY_HEADS, (QUERY_PER_KEY + 2) * HEAD_SIZE), (MODEL_WIDTH // 4) ** -0.5, 0.1875, ((0, 64), (1, 8)))
    output_weight = bell_draw(key_of[2], (KEY_HEADS * QUERY_PER_KEY * HEAD_SIZE, MODEL_WIDTH), 256 ** -0.5, 0.375, ((0, 8), (1, 64)))
    kv_pool = draw_kv_pool(jax.random.fold_in(key_of[7], 71), 0)
    lengths = draw_lengths(jax.random.fold_in(key_of[7], 71), 0)
    page_table = draw_page_table(jax.random.fold_in(key_of[7], 71), 0)
    send_slots = draw_send_slots(jax.random.fold_in(key_of[7], 71), 0)
    return {"hidden": hidden, "query_key_value_weight": query_key_value_weight, "output_weight": output_weight, "kv_pool": kv_pool, "lengths": lengths, "page_table": page_table, "send_slots": send_slots}


ROPE_BASE = 500000.0
NEG_FILL = -1e30


def rotate(vectors, angles):
    half_width = vectors.shape[-1] // 2
    first_half = vectors[..., :half_width]
    second_half = vectors[..., half_width:]
    cosine = jnp.cos(angles)
    sine_part = jnp.sin(angles)
    return jnp.concatenate([first_half * cosine - second_half * sine_part, second_half * cosine + first_half * sine_part], axis=-1)


def rope_angles(lengths, width):
    exponent = jnp.arange(width // 2, dtype=jnp.float32) * (2.0 / width)
    inverse = 1.0 / (ROPE_BASE ** exponent)
    return lengths.astype(jnp.float32)[:, None] * inverse[None, :]


def split_projection(projected_rows, lengths):
    angles = rope_angles(lengths, projected_rows.shape[-1])
    queries = rotate(projected_rows[:, :, :-2], angles[:, None, None, :]).astype(jnp.bfloat16)
    new_keys = rotate(projected_rows[:, :, -2], angles[:, None, :]).astype(jnp.bfloat16)
    new_values = projected_rows[:, :, -1].astype(jnp.bfloat16)
    return queries, new_keys, new_values


def page_stats(queries, keys, values, valid_tokens):
    score_scale = queries.shape[-1] ** -0.5
    scores = jnp.einsum("abhqd,abhtd->abhqt", queries.astype(jnp.float32), keys.astype(jnp.float32)) * score_scale
    token_mask = jnp.arange(keys.shape[-2]) < valid_tokens[:, :, None, None, None]
    masked = jnp.where(token_mask, scores, NEG_FILL)
    top_score = jnp.max(masked, axis=-1)
    weights = jnp.where(token_mask, jnp.exp(scores - top_score[..., None]), 0.0)
    weight_sum = jnp.sum(weights, axis=-1)
    rounded = lax.optimization_barrier(weights.astype(jnp.bfloat16))
    weighted_values = jnp.einsum("abhqt,abhtd->abhqd", rounded.astype(jnp.float32), values.astype(jnp.float32))
    return top_score, weight_sum, weighted_values


def reference(hidden, query_key_value_weight, output_weight, kv_pool, lengths, page_table, send_slots):
    projected_rows = jnp.dot(hidden, query_key_value_weight.reshape(MODEL_WIDTH, KEY_HEADS * (QUERY_PER_KEY + 2) * HEAD_SIZE), preferred_element_type=jnp.float32)
    projected_rows = projected_rows.reshape(TOTAL_REQUESTS, KEY_HEADS, QUERY_PER_KEY + 2, HEAD_SIZE)
    queries, new_keys, new_values = split_projection(projected_rows, lengths)
    score_scale = HEAD_SIZE ** -0.5
    self_scores = jnp.sum(queries.astype(jnp.float32) * new_keys.astype(jnp.float32)[:, :, None, :], axis=-1) * score_scale

    def single_group(group_index):
        first_row = (group_index * GROUP_REQUESTS).astype(jnp.int32)
        group_table = lax.dynamic_slice_in_dim(page_table, first_row, GROUP_REQUESTS, 0)
        group_lengths = lax.dynamic_slice_in_dim(lengths, first_row, GROUP_REQUESTS, 0)
        grouped_query_rows = lax.dynamic_slice_in_dim(queries, first_row, GROUP_REQUESTS, 0)
        group_self = lax.dynamic_slice_in_dim(self_scores, first_row, GROUP_REQUESTS, 0)
        group_values = lax.dynamic_slice_in_dim(new_values, first_row, GROUP_REQUESTS, 0)
        is_remote = group_table >= POOL_PAGES
        source = jnp.clip(group_table - POOL_PAGES, 0, REQUEST_GROUPS - 1).astype(jnp.int32)
        remote_slot = send_slots[source * REQUEST_GROUPS + group_index]
        global_index = jnp.where(is_remote, source * POOL_PAGES + remote_slot, group_index * POOL_PAGES + group_table).astype(jnp.int32)
        group_pages = kv_pool[global_index]
        places = jnp.arange(LONG_PAGES, dtype=jnp.int32)
        valid_tokens = jnp.clip(group_lengths[:, None] - places[None, :] * PAGE_TOKENS, 0, PAGE_TOKENS)
        scattered_queries = jnp.broadcast_to(grouped_query_rows[:, None], (GROUP_REQUESTS, LONG_PAGES, KEY_HEADS, QUERY_PER_KEY, HEAD_SIZE))
        page_max, page_sum, page_acc = page_stats(scattered_queries, group_pages[..., :HEAD_SIZE], group_pages[..., HEAD_SIZE:], valid_tokens)
        top_score = jnp.maximum(jnp.max(page_max, axis=1), group_self)
        factors = jnp.exp(page_max - top_score[:, None])
        self_weight = jnp.exp(group_self - top_score)
        total_weight_sum = jnp.sum(factors * page_sum, axis=1) + self_weight
        weighted_values = jnp.sum(factors[..., None] * page_acc, axis=1) + self_weight[..., None] * group_values.astype(jnp.float32)[:, :, None, :]
        return (weighted_values / total_weight_sum[..., None]).astype(jnp.bfloat16).reshape(GROUP_REQUESTS, KEY_HEADS * QUERY_PER_KEY * HEAD_SIZE)

    output_per_head = lax.map(single_group, jnp.arange(REQUEST_GROUPS, dtype=jnp.int32)).reshape(TOTAL_REQUESTS, KEY_HEADS * QUERY_PER_KEY * HEAD_SIZE)
    return jnp.dot(output_per_head, output_weight, preferred_element_type=jnp.float32).astype(jnp.bfloat16)
```

```python
import jax
import jax.numpy as jnp
from jax import lax
from jax.experimental import pallas as pl
from jax.experimental.pallas import tpu as pltpu
from jax.sharding import PartitionSpec as P

ROPE_BASE = 500000.0
NEG_FILL = -1e30
SCALE = 128 ** (-0.5)


def rotate(vectors, angles):
    half_width = vectors.shape[-1] // 2
    first_half = vectors[..., :half_width]
    second_half = vectors[..., half_width:]
    cosine = jnp.cos(angles)
    sine_part = jnp.sin(angles)
    return jnp.concatenate(
        [
            first_half * cosine - second_half * sine_part,
            second_half * cosine + first_half * sine_part,
        ],
        axis=-1,
    )


def rope_angles(lengths, width):
    exponent = jnp.arange(width // 2, dtype=jnp.float32) * (2.0 / width)
    inverse = 1.0 / ROPE_BASE**exponent
    return lengths.astype(jnp.float32)[:, None] * inverse[None, :]


def remote(src, dst, send, recv, req, head=None):
    where = {"req": req} if head is None else {"req": req, "head": head}
    return pltpu.make_async_remote_copy(
        src_ref=src, dst_ref=dst, send_sem=send, recv_sem=recv,
        device_id=where, device_id_type=pl.DeviceIdType.MESH,
    )


def greet(barrier, req, head=None):
    where = {"req": req} if head is None else {"req": req, "head": head}
    pl.semaphore_signal(barrier, inc=1, device_id=where, device_id_type=pl.DeviceIdType.MESH)


def for_each(start, stop, body):
    def step(i, carry):
        body(i)
        return carry
    lax.fori_loop(start, stop, step, 0)


def place(req):
    return req // 16, lax.rem(req // 2, 8), lax.rem(req, 2)


def project_kernel(
    pay_ref, wo_ref, out_ref, wg_ref, gathered, partial, parts, s1, r1, s2, r2, s3, r3, own
):
    req = lax.axis_index("req")
    x, y, c = place(req)
    xc = x * 2 + c
    yc = y * 2 + c

    def at_xc(i):
        return (i // 2) * 16 + y * 2 + lax.rem(i, 2)

    barrier = pltpu.get_barrier_semaphore()
    for_each(1, 8, lambda k: greet(barrier, at_xc(lax.rem(xc + k, 8))))
    for_each(1, 16, lambda k: greet(barrier, x * 16 + lax.rem(yc + k, 16)))
    own_pay = pltpu.make_async_copy(pay_ref.at[xc], gathered.at[xc], own.at[0])
    own_wo = pltpu.make_async_copy(wo_ref, wg_ref.at[xc], own.at[1])
    own_pay.start()
    own_wo.start()
    pl.semaphore_wait(barrier, 22)

    def send_pay(k):
        peer = lax.rem(xc + k, 8)
        return remote(pay_ref.at[peer], gathered.at[xc], s1.at[k], r1.at[k], at_xc(peer))

    def send_wo(k):
        peer = lax.rem(xc + k, 8)
        return remote(wo_ref, wg_ref.at[xc], s3.at[k], r3.at[k], at_xc(peer))

    def send_part(k):
        peer = lax.rem(yc + k, 16)
        return remote(partial.at[peer], parts.at[yc], s2.at[k], r2.at[k], x * 16 + peer)

    for_each(1, 8, lambda k: send_pay(k).start())
    own_pay.wait()
    for_each(1, 8, lambda k: send_pay(k).wait_recv())
    for_each(1, 8, lambda k: send_wo(k).start())
    rows = gathered[:, :, :128].reshape(512, 128)
    cols = gathered[:, :, 128:].reshape(512, 384)
    sums = lax.dot_general(
        rows, cols, (((0,), (0,)), ((), ())), preferred_element_type=jnp.float32
    )
    partial[...] = sums.reshape(16, 8, 384)
    own_part = pltpu.make_async_copy(partial.at[yc], parts.at[yc], own.at[0])
    own_part.start()
    for_each(1, 16, lambda k: send_part(k).start())
    own_part.wait()
    for_each(1, 16, lambda k: send_part(k).wait_recv())
    total = parts[0:2]
    for i in range(1, 8):
        total = total + parts[2 * i : 2 * i + 2]
    out_ref[...] = total
    own_wo.wait()
    for_each(1, 8, lambda k: send_pay(k).wait_send())
    for_each(1, 16, lambda k: send_part(k).wait_send())
    for_each(1, 8, lambda k: send_wo(k).wait())


def split_three(v):
    high = v.astype(jnp.bfloat16).astype(jnp.float32)
    rest = v - high
    mid = rest.astype(jnp.bfloat16).astype(jnp.float32)
    return high, mid, rest - mid


def attend_kernel(
    slots_ref, msg_ref, q_ref, valid_ref, kv_ref, back_ref, acc_ref, max_ref, sum_ref,
    pages, asked, scores, reply, s1, r1, s2, r2, own,
):
    me = lax.axis_index("req")
    load = pltpu.make_async_copy(kv_ref, pages, own.at[0])
    load.start()
    barrier = pltpu.get_barrier_semaphore()
    for_each(1, 64, lambda k: greet(barrier, lax.rem(me + k, 64)))
    own_ask = pltpu.make_async_copy(msg_ref.at[me], asked.at[me], own.at[1])
    own_ask.start()
    pl.semaphore_wait(barrier, 63)

    def ask(k):
        peer = lax.rem(me + k, 64)
        return remote(msg_ref.at[peer], asked.at[me], s1.at[k], r1.at[k], peer)

    def answer(k):
        peer = lax.rem(me + k, 64)
        return remote(reply.at[peer], back_ref.at[me], s2.at[k], r2.at[k], peer)

    for_each(1, 64, lambda k: ask(k).start())
    load.wait()

    lane = lax.broadcasted_iota(jnp.int32, (32, 128), 1)
    queries = q_ref[...]
    valid = valid_ref[...]

    def score(e, top):
        s = lax.dot_general(
            queries, pages[e, :, 0:128], (((1,), (1,)), ((), ())),
            preferred_element_type=jnp.float32,
        ) * SCALE
        tokens = jnp.sum(jnp.where(lane == e, valid, 0), axis=1, keepdims=True)
        s = jnp.where(lane < tokens, s, NEG_FILL)
        scores[e] = s
        return jnp.maximum(top, s)

    top = lax.fori_loop(0, 64, score, jnp.full((32, 128), NEG_FILL, jnp.float32), unroll=4)
    top = jnp.broadcast_to(jnp.max(top, axis=1, keepdims=True), (32, 128))

    def gather(e, carry):
        acc, total = carry
        s = scores[e]
        w = jnp.where(s > 0.5 * NEG_FILL, jnp.exp(s - top), 0.0)
        acc = acc + jnp.dot(
            w.astype(jnp.bfloat16), pages[e, :, 128:256], preferred_element_type=jnp.float32
        )
        return acc, total + w

    zero = jnp.zeros((32, 128), jnp.float32)
    acc, total = lax.fori_loop(0, 64, gather, (zero, zero), unroll=4)
    acc_ref[...] = acc
    max_ref[...] = top
    sum_ref[...] = jnp.broadcast_to(jnp.sum(total, axis=1, keepdims=True), (32, 128))

    own_ask.wait()
    for_each(1, 64, lambda k: ask(k).wait_recv())

    lane8 = lax.broadcasted_iota(jnp.int32, (8, 128), 1)
    row8 = lax.broadcasted_iota(jnp.int32, (8, 128), 0)

    def serve(g, carry):
        slot = slots_ref[g]
        query = asked[g].astype(jnp.float32)
        tokens = query[4:5, 0:1]
        query = jnp.where(row8 < 4, query, pltpu.roll(query, 4, 0)).astype(jnp.bfloat16)
        s = lax.dot_general(
            query, pages[slot, :, 0:128], (((1,), (1,)), ((), ())),
            preferred_element_type=jnp.float32,
        ) * SCALE
        mask = lane8.astype(jnp.float32) < tokens
        s = jnp.where(mask, s, NEG_FILL)
        m = jnp.max(s, axis=1, keepdims=True)
        w = jnp.where(mask, jnp.exp(s - m), 0.0)
        l = jnp.sum(w, axis=1, keepdims=True)
        a = jnp.dot(
            w.astype(jnp.bfloat16), pages[slot, :, 128:256], preferred_element_type=jnp.float32
        )
        m0, m1, m2 = split_three(jnp.broadcast_to(m, (8, 128)))
        l0, l1, l2 = split_three(jnp.broadcast_to(l, (8, 128)))
        stats = jnp.where(lane8 < 16, m0, jnp.where(lane8 < 32, m1, jnp.where(lane8 < 48, m2,
                jnp.where(lane8 < 64, l0, jnp.where(lane8 < 80, l1, l2)))))
        reply[g] = jnp.where(row8 < 4, a, stats).astype(jnp.bfloat16)
        return carry

    lax.fori_loop(0, 64, serve, 0, unroll=4)
    own_answer = pltpu.make_async_copy(reply.at[me], back_ref.at[me], own.at[0])
    own_answer.start()
    for_each(1, 64, lambda k: answer(k).start())
    own_answer.wait()
    for_each(1, 64, lambda k: answer(k).wait_recv())
    for_each(1, 64, lambda k: ask(k).wait_send())
    for_each(1, 64, lambda k: answer(k).wait_send())


def output_kernel(heads_ref, wg_ref, out_ref, rows, partial, parts, s1, r1, s2, r2, own):
    req = lax.axis_index("req")
    z = lax.axis_index("head")
    x, y, c = place(req)
    mine = (z // 2) == x

    def dest(k):
        return (k // 4) * 16 + y * 2 + lax.rem(k // 2, 2), x * 2 + lax.rem(k, 2)

    def origin(k):
        return (z // 2) * 16 + y * 2 + k // 8, lax.rem(k, 8)

    def is_me(pair):
        return jnp.logical_and(pair[0] == req, pair[1] == z)

    barrier = pltpu.get_barrier_semaphore()
    for_each(1, 8, lambda k: greet(barrier, x * 16 + lax.rem(y + k, 8) * 2 + c))

    def hello(k):
        @pl.when(jnp.logical_not(is_me(origin(k))))
        def _():
            greet(barrier, *origin(k))

    for_each(0, 16, hello)
    own_rows = pltpu.make_async_copy(heads_ref, rows.at[y], own.at[0])
    own_rows.start()

    @pl.when(mine)
    def _():
        pl.semaphore_wait(barrier, 22)

    @pl.when(jnp.logical_not(mine))
    def _():
        pl.semaphore_wait(barrier, 23)

    def send_rows(k):
        peer = x * 16 + lax.rem(y + k, 8) * 2 + c
        return remote(heads_ref, rows.at[y], s1.at[k], r1.at[k], peer)

    for_each(1, 8, lambda k: send_rows(k).start())
    own_rows.wait()
    for_each(1, 8, lambda k: send_rows(k).wait_recv())
    heads = rows[...].astype(jnp.float32).reshape(64, 512).astype(jnp.bfloat16)
    for i in range(8):
        tile = lax.dot_general(
            heads, wg_ref[i], (((1,), (1,)), ((), ())), preferred_element_type=jnp.float32
        ).astype(jnp.bfloat16)
        partial[2 * i] = tile[0:32]
        partial[2 * i + 1] = tile[32:64]

    spot = c * 8 + z

    def push(k):
        return remote(partial.at[k], parts.at[spot], s2.at[k], r2.at[spot], *dest(k))

    def send(k):
        @pl.when(is_me(dest(k)))
        def _():
            pltpu.make_async_copy(partial.at[k], parts.at[spot], r2.at[spot]).start()

        @pl.when(jnp.logical_not(is_me(dest(k))))
        def _():
            push(k).start()

    for_each(0, 16, send)

    def receive(k):
        pltpu.make_async_copy(parts.at[k], parts.at[k], r2.at[k]).wait()

    for_each(0, 16, receive)
    for j in range(2):
        total = parts[8 * j].astype(jnp.float32)
        for h in range(1, 8):
            total = total + parts[8 * j + h].astype(jnp.float32)
        out_ref[j] = total
    for_each(1, 8, lambda k: send_rows(k).wait_send())

    def sent(k):
        @pl.when(jnp.logical_not(is_me(dest(k))))
        def _():
            push(k).wait_send()

    for_each(0, 16, sent)


def vmem():
    return pl.BlockSpec(memory_space=pltpu.VMEM)


def params(ident):
    return pltpu.CompilerParams(collective_id=ident, has_side_effects=True)


def dma(count):
    return pltpu.SemaphoreType.DMA((count,))


def shards(hidden, query_key_value_weight, output_weight, kv_pool, lengths, page_table, send_slots):
    bf16, f32 = jnp.bfloat16, jnp.float32
    hidden_t = hidden.T.reshape(64, 4, 128).transpose(1, 0, 2)
    weight = query_key_value_weight.reshape(64, 2, 384).transpose(1, 0, 2)
    payload = jnp.concatenate(
        [
            jnp.broadcast_to(hidden_t[:, None], (4, 2, 64, 128)),
            jnp.broadcast_to(weight[None], (4, 2, 64, 384)),
        ],
        axis=-1,
    ).reshape(8, 64, 512)
    projected, out_cols = pl.pallas_call(
        project_kernel,
        out_shape=(
            jax.ShapeDtypeStruct((2, 8, 384), f32),
            jax.ShapeDtypeStruct((8, 64, 512), bf16),
        ),
        in_specs=[vmem()] * 2,
        out_specs=(vmem(), vmem()),
        scratch_shapes=[
            pltpu.VMEM((8, 64, 512), bf16),
            pltpu.VMEM((16, 8, 384), f32),
            pltpu.VMEM((16, 8, 384), f32),
            dma(8), dma(8), dma(16), dma(16), dma(8), dma(8), dma(2),
        ],
        compiler_params=params(1),
    )(payload, output_weight.T)

    rows = projected.transpose(1, 0, 2).reshape(8, 6, 128)
    angles = rope_angles(lengths, 128)
    queries = rotate(rows[:, :4], angles[:, None, :]).astype(bf16)
    new_keys = rotate(rows[:, 4], angles).astype(bf16)
    new_values = rows[:, 5].astype(bf16)
    self_scores = (
        jnp.sum(queries.astype(f32) * new_keys.astype(f32)[:, None, :], axis=-1) * SCALE
    )

    places = jnp.arange(16, dtype=jnp.int32)
    is_live = places[None, :] * 128 < lengths[:, None]
    tokens_in = jnp.clip(lengths[:, None] - places[None, :] * 128, 0, 128)
    hits = (page_table[:, :, None] == jnp.arange(128, dtype=jnp.int32)) & is_live[:, :, None]
    valid = jnp.sum(jnp.where(hits, tokens_in[:, :, None], 0), axis=1)
    owned = valid[:, 64:] > 0
    asking = jnp.einsum(
        "rs,rqd->sqd", owned.astype(bf16), queries, preferred_element_type=f32
    ).astype(bf16)
    tokens = jnp.sum(valid[:, 64:], axis=0).astype(bf16)
    message = jnp.concatenate(
        [asking, jnp.broadcast_to(tokens[:, None, None], (64, 4, 128))], axis=1
    )
    back, acc, top, total = pl.pallas_call(
        attend_kernel,
        out_shape=(
            jax.ShapeDtypeStruct((64, 8, 128), bf16),
            jax.ShapeDtypeStruct((32, 128), f32),
            jax.ShapeDtypeStruct((32, 128), f32),
            jax.ShapeDtypeStruct((32, 128), f32),
        ),
        in_specs=[
            pl.BlockSpec(memory_space=pltpu.SMEM), vmem(), vmem(), vmem(),
            pl.BlockSpec(memory_space=pl.ANY),
        ],
        out_specs=(vmem(), vmem(), vmem(), vmem()),
        scratch_shapes=[
            pltpu.VMEM((64, 128, 256), bf16),
            pltpu.VMEM((64, 8, 128), bf16),
            pltpu.VMEM((64, 32, 128), f32),
            pltpu.VMEM((64, 8, 128), bf16),
            dma(64), dma(64), dma(64), dma(64), dma(2),
        ],
        compiler_params=params(2),
    )(
        send_slots, message, queries.transpose(1, 0, 2).reshape(32, 128),
        jnp.tile(valid, (4, 1)), kv_pool.reshape(64, 128, 256),
    )

    far = back[:, :4].astype(f32)
    stats = back[:, 4:].astype(f32)
    far_max = stats[:, :, 0] + stats[:, :, 16] + stats[:, :, 32]
    far_sum = stats[:, :, 48] + stats[:, :, 64] + stats[:, :, 80]
    near = acc.reshape(4, 8, 128).transpose(1, 0, 2)
    near_max = top[:, 0].reshape(4, 8).T
    near_sum = total[:, 0].reshape(4, 8).T
    picked = owned[:, :, None]
    peak = jnp.max(jnp.where(picked, far_max[None], NEG_FILL), axis=1)
    peak = jnp.maximum(jnp.maximum(peak, near_max), self_scores)
    factors = jnp.where(picked, jnp.exp(jnp.minimum(far_max[None] - peak[:, None], 0.0)), 0.0)
    near_factor = jnp.exp(near_max - peak)
    self_factor = jnp.exp(self_scores - peak)
    weight_sum = jnp.sum(factors * far_sum[None], axis=1) + near_factor * near_sum + self_factor
    weighted = (
        jnp.einsum("rsq,sqd->rqd", factors, far, precision=lax.Precision.HIGHEST)
        + near_factor[..., None] * near
        + self_factor[..., None] * new_values.astype(f32)[:, None, :]
    )
    heads = (weighted / weight_sum[..., None]).astype(bf16).reshape(8, 512)

    summed = pl.pallas_call(
        output_kernel,
        out_shape=jax.ShapeDtypeStruct((2, 32, 64), f32),
        in_specs=[vmem()] * 2,
        out_specs=vmem(),
        scratch_shapes=[
            pltpu.VMEM((8, 8, 512), bf16),
            pltpu.VMEM((16, 32, 64), bf16),
            pltpu.VMEM((16, 32, 64), bf16),
            dma(8), dma(8), dma(16), dma(16), dma(1),
        ],
        compiler_params=params(3),
    )(heads, out_cols)
    return (
        summed.reshape(2, 4, 8, 64).transpose(1, 0, 2, 3).reshape(64, 64).astype(bf16)
    )


def solution(mesh):
    return jax.shard_map(
        shards,
        mesh=mesh,
        in_specs=(
            P(None, "req"),
            P("req", "head", None),
            P("head", "req"),
            P("req", "head", None, None),
            P("req"),
            P("req", None),
            P("req"),
        ),
        out_specs=P("head", "req"),
        check_vma=False,
    )
```

```python
import jax
import jax.numpy as jnp
from jax import lax
from jax.experimental import pallas as pl
from jax.experimental.pallas import tpu as pltpu
from jax.sharding import PartitionSpec as P

ROPE_BASE = 500000.0
NEG_FILL = -1e30
SCALE = 128 ** (-0.5)


def rope_angles(lengths, width):
    exponent = jnp.arange(width // 2, dtype=jnp.float32) * (2.0 / width)
    inverse = 1.0 / ROPE_BASE**exponent
    return lengths.astype(jnp.float32)[:, None] * inverse[None, :]


def remote(src, dst, send, recv, req, head=None):
    where = {"req": req} if head is None else {"req": req, "head": head}
    return pltpu.make_async_remote_copy(
        src_ref=src, dst_ref=dst, send_sem=send, recv_sem=recv,
        device_id=where, device_id_type=pl.DeviceIdType.MESH,
    )


def greet(barrier, req, head=None):
    where = {"req": req} if head is None else {"req": req, "head": head}
    pl.semaphore_signal(barrier, inc=1, device_id=where, device_id_type=pl.DeviceIdType.MESH)


def for_each(start, stop, body):
    def step(i, carry):
        body(i)
        return carry
    lax.fori_loop(start, stop, step, 0)


def place(req):
    return req // 16, lax.rem(req // 2, 8), lax.rem(req, 2)


def split_three(v):
    high = v.astype(jnp.bfloat16).astype(jnp.float32)
    rest = v - high
    mid = rest.astype(jnp.bfloat16).astype(jnp.float32)
    return high, mid, rest - mid


def dot_nt(a, b):
    return lax.dot_general(a, b, (((1,), (1,)), ((), ())), preferred_element_type=jnp.float32)


def dot_tn(a, b):
    return lax.dot_general(a, b, (((0,), (0,)), ((), ())), preferred_element_type=jnp.float32)


def layer_kernel(
    slots_ref, lengths_ref, table_ref, cos_ref, sin_ref, pay_ref, wo_ref, kv_ref, out_ref,
    gathered, wide, partial, parts, pages, ask_buf, asked, scores, reply, back, heads_buf, rows,
    piece, pieces, own, s1, r1, s2, r2, s3, r3, s4, r4, s5, r5, s6, r6, s7, r7,
):
    bf16, f32 = jnp.bfloat16, jnp.float32
    req = lax.axis_index("req")
    z = lax.axis_index("head")
    x, y, c = place(req)
    xc = x * 2 + c
    yc = y * 2 + c
    mine = (z // 2) == x
    spot = c * 8 + z

    def at_xc(i):
        return (i // 2) * 16 + y * 2 + lax.rem(i, 2)

    def dest(k):
        return (k // 4) * 16 + y * 2 + lax.rem(k // 2, 2), x * 2 + lax.rem(k, 2)

    def origin(k):
        return (z // 2) * 16 + y * 2 + k // 8, lax.rem(k, 8)

    def is_me(pair):
        return jnp.logical_and(pair[0] == req, pair[1] == z)

    barrier = pltpu.get_barrier_semaphore()
    for_each(1, 64, lambda k: greet(barrier, lax.rem(req + k, 64)))

    def hello(k):
        @pl.when(jnp.logical_not(is_me(origin(k))))
        def _():
            greet(barrier, *origin(k))

    for_each(0, 16, hello)
    load = pltpu.make_async_copy(kv_ref, pages, own.at[0])
    load.start()
    own_pay = pltpu.make_async_copy(pay_ref.at[xc], gathered.at[xc], own.at[1])
    own_wo = pltpu.make_async_copy(wo_ref, wide.at[xc], own.at[2])
    own_pay.start()
    own_wo.start()

    row = lax.broadcasted_iota(jnp.int32, (8, 128), 0)
    lane = lax.broadcasted_iota(jnp.int32, (8, 128), 1)
    long = jnp.zeros((8, 128), jnp.int32)
    for i in range(8):
        long = jnp.where(row == i, lengths_ref[i], long)
    table = table_ref[...]
    valid = jnp.zeros((8, 128), jnp.int32)
    for p in range(16):
        tokens = jnp.clip(long - p * 128, 0, 128)
        valid = valid + jnp.where(table[:, p : p + 1] == lane, tokens, 0)
    spread = (
        lax.broadcasted_iota(jnp.int32, (128, 512), 0) - 64
        == lax.broadcasted_iota(jnp.int32, (128, 512), 1) // 8
    )
    wanted = jnp.dot(
        valid.astype(f32).astype(bf16),
        jnp.where(spread, 1.0, 0.0).astype(bf16),
        preferred_element_type=f32,
    )
    part8 = lax.rem(lax.broadcasted_iota(jnp.int32, (8, 512), 1), 8)
    owned = [
        jnp.where(jnp.logical_and(wanted > 0.0, part8 == q), 1.0, 0.0) for q in range(4)
    ]
    asking = owned + [jnp.where(part8 >= 4, wanted, 0.0)]
    owned = jnp.concatenate(owned, axis=0)
    asking = jnp.concatenate(asking, axis=0)
    valid = jnp.concatenate([valid] * 4, axis=0)

    @pl.when(mine)
    def _():
        pl.semaphore_wait(barrier, 63 + 15)

    @pl.when(jnp.logical_not(mine))
    def _():
        pl.semaphore_wait(barrier, 63 + 16)

    def send_pay(k):
        peer = lax.rem(xc + k, 8)
        return remote(pay_ref.at[peer], gathered.at[xc], s1.at[k], r1.at[k], at_xc(peer))

    def send_part(k):
        peer = lax.rem(yc + k, 16)
        return remote(partial.at[peer], parts.at[yc], s2.at[k], r2.at[k], x * 16 + peer)

    def send_wo(k):
        peer = lax.rem(xc + k, 8)
        return remote(wo_ref, wide.at[xc], s3.at[k], r3.at[k], at_xc(peer))

    def ask(k):
        peer = lax.rem(req + k, 64)
        return remote(ask_buf.at[peer], asked.at[req], s4.at[k], r4.at[k], peer)

    def answer(k):
        peer = lax.rem(req - k + 64, 64)
        return remote(reply.at[peer], back.at[req], s5.at[k], r5.at[k], peer)

    def send_rows(k):
        peer = x * 16 + lax.rem(y + k, 8) * 2 + c
        return remote(heads_buf, rows.at[y], s6.at[k], r6.at[k], peer)

    def push(k):
        return remote(piece.at[k], pieces.at[spot], s7.at[k], r7.at[spot], *dest(k))

    for_each(1, 8, lambda k: send_pay(k).start())
    own_pay.wait()
    for_each(1, 8, lambda k: send_pay(k).wait_recv())
    for_each(1, 8, lambda k: send_wo(k).start())
    sums = dot_tn(
        gathered[:, :, :128].reshape(512, 128), gathered[:, :, 128:].reshape(512, 384)
    )
    partial[...] = sums.reshape(16, 8, 384)
    own_part = pltpu.make_async_copy(partial.at[yc], parts.at[yc], own.at[1])
    own_part.start()
    for_each(1, 16, lambda k: send_part(k).start())
    own_part.wait()
    for_each(1, 16, lambda k: send_part(k).wait_recv())
    total = parts[0:2]
    for i in range(1, 8):
        total = total + parts[2 * i : 2 * i + 2]
    made = [total[h // 3, :, 128 * (h % 3) : 128 * (h % 3) + 128] for h in range(6)]
    cosine, sine = cos_ref[...], sin_ref[...]

    def turn(v):
        return (v * cosine + pltpu.roll(v, 64, 1) * sine).astype(bf16).astype(f32)

    queries = jnp.concatenate([turn(made[q]) for q in range(4)], axis=0)
    new_keys = jnp.concatenate([turn(made[4])] * 4, axis=0)
    new_values = jnp.concatenate([made[5].astype(bf16).astype(f32)] * 4, axis=0)
    self_scores = jnp.sum(queries * new_keys, axis=1, keepdims=True) * SCALE
    ask_rows = dot_tn(
        asking.astype(bf16),
        jnp.concatenate([queries, jnp.ones((8, 128), f32)], axis=0).astype(bf16),
    )
    ask_buf[...] = ask_rows.reshape(64, 8, 128).astype(bf16)
    own_ask = pltpu.make_async_copy(ask_buf.at[req], asked.at[req], own.at[1])
    own_ask.start()
    for_each(1, 64, lambda k: ask(k).start())
    load.wait()

    lane32 = lax.broadcasted_iota(jnp.int32, (32, 128), 1)
    queries = queries.astype(bf16)

    def score(e, top):
        s = dot_nt(queries, pages[e, :, 0:128]) * SCALE
        tokens = jnp.sum(jnp.where(lane32 == e, valid, 0), axis=1, keepdims=True)
        s = jnp.where(lane32 < tokens, s, NEG_FILL)
        scores[e] = s
        return jnp.maximum(top, s)

    near_max = lax.fori_loop(0, 64, score, jnp.full((32, 128), NEG_FILL, f32), unroll=8)
    near_max = jnp.max(near_max, axis=1, keepdims=True)

    def gather(e, carry):
        acc, weight = carry
        s = scores[e]
        w = jnp.where(s > 0.5 * NEG_FILL, jnp.exp(s - near_max), 0.0)
        return acc + jnp.dot(w.astype(bf16), pages[e, :, 128:256], preferred_element_type=f32), weight + w

    zero = jnp.zeros((32, 128), f32)
    near, near_sum = lax.fori_loop(0, 64, gather, (zero, zero), unroll=8)
    near_sum = jnp.sum(near_sum, axis=1, keepdims=True)

    own_ask.wait()
    batch = 16
    row3 = lax.broadcasted_iota(jnp.int32, (batch, 8, 128), 1)
    lane3 = lax.broadcasted_iota(jnp.int32, (batch, 8, 128), 2)
    own_answer = pltpu.make_async_copy(reply.at[req], back.at[req], own.at[0])

    def serve(j, carry):
        first = j * batch

        def heard(k):
            @pl.when(k > 0)
            def _():
                ask(k).wait_recv()

        def tell(k):
            @pl.when(k > 0)
            def _():
                answer(k).start()

        for_each(first, first + batch, heard)
        sources = [lax.rem(req - first - i + 64, 64) for i in range(batch)]
        slots = [slots_ref[g] for g in sources]
        query, limit = [], []
        for g in sources:
            both = asked[g].astype(f32)
            other = pltpu.roll(both, 4, 0)
            query.append(jnp.where(row < 4, both, other).astype(bf16))
            limit.append(jnp.where(row < 4, other, both))
        limit = jnp.stack(limit)
        s = jnp.stack([dot_nt(query[i], pages[slots[i], :, 0:128]) for i in range(batch)]) * SCALE
        mask = lane3.astype(f32) < limit
        s = jnp.where(mask, s, NEG_FILL)
        m = jnp.max(s, axis=2, keepdims=True)
        w = jnp.where(mask, jnp.exp(s - m), 0.0)
        l = jnp.sum(w, axis=2, keepdims=True)
        m0, m1, m2 = split_three(jnp.broadcast_to(m, s.shape))
        l0, l1, l2 = split_three(jnp.broadcast_to(l, s.shape))
        stats = jnp.where(lane3 < 16, m0, jnp.where(lane3 < 32, m1, jnp.where(lane3 < 48, m2,
                jnp.where(lane3 < 64, l0, jnp.where(lane3 < 80, l1, l2)))))
        for i in range(batch):
            a = jnp.dot(
                w[i].astype(bf16), pages[slots[i], :, 128:256], preferred_element_type=f32
            )
            reply[sources[i]] = jnp.where(row < 4, a, stats[i]).astype(bf16)
        for_each(first, first + batch, tell)
        return carry

    lax.fori_loop(0, 64 // batch, serve, 0)
    own_answer.start()
    own_answer.wait()
    for_each(1, 64, lambda k: answer(k).wait_recv())

    far = back[...].astype(f32).reshape(512, 128).astype(bf16)
    pick_max = jnp.logical_and(lane < 48, lax.rem(lane, 16) == 0)
    pick_sum = jnp.logical_and(
        jnp.logical_and(lane >= 48, lane < 96), lax.rem(lane, 16) == 0
    )
    far_max = dot_nt(jnp.where(pick_max, 1.0, 0.0).astype(bf16), far)
    far_sum = dot_nt(jnp.where(pick_sum, 1.0, 0.0).astype(bf16), far)
    far_max = jnp.concatenate([pltpu.roll(far_max, 508, 1)] * 4, axis=0)
    far_sum = jnp.concatenate([pltpu.roll(far_sum, 508, 1)] * 4, axis=0)
    picked = owned > 0.5
    peak = jnp.max(jnp.where(picked, far_max, NEG_FILL), axis=1, keepdims=True)
    peak = jnp.maximum(jnp.maximum(peak, near_max), self_scores)
    factors = jnp.where(picked, jnp.exp(jnp.minimum(far_max - peak, 0.0)), 0.0)
    near_factor = jnp.exp(near_max - peak)
    self_factor = jnp.exp(self_scores - peak)
    weight_sum = (
        jnp.sum(jnp.where(picked, factors * far_sum, 0.0), axis=1, keepdims=True)
        + near_factor * near_sum + self_factor
    )
    high = factors.astype(bf16)
    low = (factors - high.astype(f32)).astype(bf16)
    weighted = (
        jnp.dot(high, far, preferred_element_type=f32)
        + jnp.dot(low, far, preferred_element_type=f32)
        + near_factor * near + self_factor * new_values
    )
    heads_buf[...] = (weighted / weight_sum).astype(bf16)

    own_rows = pltpu.make_async_copy(heads_buf, rows.at[y], own.at[0])
    own_rows.start()
    for_each(1, 8, lambda k: send_rows(k).start())
    own_wo.wait()
    for_each(1, 8, lambda k: send_wo(k).wait_recv())
    own_rows.wait()
    for_each(1, 8, lambda k: send_rows(k).wait_recv())
    heads = rows[...].astype(f32)
    heads = jnp.concatenate(
        [heads[:, 8 * q : 8 * q + 8].reshape(64, 128) for q in range(4)], axis=1
    ).astype(bf16)
    for i in range(8):
        tile = dot_nt(heads, wide[i]).astype(bf16)
        piece[2 * i] = tile[0:32]
        piece[2 * i + 1] = tile[32:64]

    def send(k):
        @pl.when(is_me(dest(k)))
        def _():
            pltpu.make_async_copy(piece.at[k], pieces.at[spot], r7.at[spot]).start()

        @pl.when(jnp.logical_not(is_me(dest(k))))
        def _():
            push(k).start()

    for_each(0, 16, send)
    for_each(1, 64, lambda k: ask(k).wait_send())
    for_each(1, 64, lambda k: answer(k).wait_send())
    for_each(1, 8, lambda k: send_pay(k).wait_send())
    for_each(1, 16, lambda k: send_part(k).wait_send())
    for_each(1, 8, lambda k: send_wo(k).wait_send())
    for_each(1, 8, lambda k: send_rows(k).wait_send())

    def receive(k):
        pltpu.make_async_copy(pieces.at[k], pieces.at[k], r7.at[k]).wait()

    for_each(0, 16, receive)
    totals = []
    for j in range(2):
        total = pieces[8 * j].astype(f32)
        for h in range(1, 8):
            total = total + pieces[8 * j + h].astype(f32)
        totals.append(total)
    out_ref[...] = jnp.concatenate(
        [totals[j][8 * i : 8 * i + 8] for i in range(4) for j in range(2)], axis=0
    ).astype(bf16)

    def sent(k):
        @pl.when(jnp.logical_not(is_me(dest(k))))
        def _():
            push(k).wait_send()

    for_each(0, 16, sent)


def vmem():
    return pl.BlockSpec(memory_space=pltpu.VMEM)


def params(ident):
    return pltpu.CompilerParams(collective_id=ident, has_side_effects=True)


def dma(count):
    return pltpu.SemaphoreType.DMA((count,))


def shards(hidden, query_key_value_weight, output_weight, kv_pool, lengths, page_table, send_slots):
    bf16, f32 = jnp.bfloat16, jnp.float32
    hidden_t = hidden.T.reshape(64, 4, 128).transpose(1, 0, 2)
    weight = query_key_value_weight.reshape(64, 2, 384).transpose(1, 0, 2)
    payload = jnp.concatenate(
        [
            jnp.broadcast_to(hidden_t[:, None], (4, 2, 64, 128)),
            jnp.broadcast_to(weight[None], (4, 2, 64, 384)),
        ],
        axis=-1,
    ).reshape(8, 64, 512)
    angles = rope_angles(lengths, 128)
    angles = jnp.concatenate([angles, angles], axis=1)
    sign = jnp.where(jnp.arange(128) < 64, -1.0, 1.0).astype(f32)
    smem = pl.BlockSpec(memory_space=pltpu.SMEM)
    return pl.pallas_call(
        layer_kernel,
        out_shape=jax.ShapeDtypeStruct((64, 64), bf16),
        in_specs=[smem, smem] + [vmem()] * 5 + [pl.BlockSpec(memory_space=pl.ANY)],
        out_specs=vmem(),
        scratch_shapes=[
            pltpu.VMEM((8, 64, 512), bf16),
            pltpu.VMEM((8, 64, 512), bf16),
            pltpu.VMEM((16, 8, 384), f32),
            pltpu.VMEM((16, 8, 384), f32),
            pltpu.VMEM((64, 128, 256), bf16),
            pltpu.VMEM((64, 8, 128), bf16),
            pltpu.VMEM((64, 8, 128), bf16),
            pltpu.VMEM((64, 32, 128), f32),
            pltpu.VMEM((64, 8, 128), bf16),
            pltpu.VMEM((64, 8, 128), bf16),
            pltpu.VMEM((32, 128), bf16),
            pltpu.VMEM((8, 32, 128), bf16),
            pltpu.VMEM((16, 32, 64), bf16),
            pltpu.VMEM((16, 32, 64), bf16),
            dma(3), dma(8), dma(8), dma(16), dma(16), dma(8), dma(8), dma(64), dma(64),
            dma(64), dma(64), dma(8), dma(8), dma(16), dma(16),
        ],
        compiler_params=params(1),
    )(
        send_slots, lengths, page_table, jnp.cos(angles), jnp.sin(angles) * sign,
        payload, output_weight.T, kv_pool.reshape(64, 128, 256),
    )


def solution(mesh):
    return jax.shard_map(
        shards,
        mesh=mesh,
        in_specs=(
            P(None, "req"),
            P("req", "head", None),
            P("head", "req"),
            P("req", "head", None, None),
            P("req"),
            P("req", None),
            P("req"),
        ),
        out_specs=P("head", "req"),
        check_vma=False,
    )
```

```python
import jax
import jax.numpy as jnp
import numpy as np
from jax import lax
from jax.experimental import pallas as pl
from jax.experimental.pallas import tpu as pltpu
from jax.sharding import PartitionSpec as P

ROPE_BASE = 500000.0
NEG_FILL = -1e30
SCALE = 128 ** (-0.5)


def remote(src, dst, send, recv, req, head=None):
    where = {"req": req} if head is None else {"req": req, "head": head}
    return pltpu.make_async_remote_copy(
        src_ref=src, dst_ref=dst, send_sem=send, recv_sem=recv,
        device_id=where, device_id_type=pl.DeviceIdType.MESH,
    )


def greet(barrier, req, head=None):
    where = {"req": req} if head is None else {"req": req, "head": head}
    pl.semaphore_signal(barrier, inc=1, device_id=where, device_id_type=pl.DeviceIdType.MESH)


def for_each(start, stop, body):
    def step(i, carry):
        body(i)
        return carry
    lax.fori_loop(start, stop, step, 0)


def place(req):
    return req // 16, lax.rem(req // 2, 8), lax.rem(req, 2)


def split_three(v):
    high = v.astype(jnp.bfloat16).astype(jnp.float32)
    rest = v - high
    mid = rest.astype(jnp.bfloat16).astype(jnp.float32)
    return high, mid, rest - mid


def dot_nt(a, b):
    return lax.dot_general(a, b, (((1,), (1,)), ((), ())), preferred_element_type=jnp.float32)


def dot_tn(a, b):
    return lax.dot_general(a, b, (((0,), (0,)), ((), ())), preferred_element_type=jnp.float32)


def layer_kernel(
    slots_ref, lengths_ref, table_ref, base_ref, hid_ref, w_ref, wo_ref, kv_ref, out_ref,
    gathered, weights, wide, partial, parts, pages, limits, ask_buf, asked, scores, reply, back, heads_buf, rows,
    piece, pieces, own, s1, r1, s2, r2, s3, r3, s4, r4, s5, r5, s6, r6, s7, r7,
    s8, r8,
):
    bf16, f32 = jnp.bfloat16, jnp.float32
    req = lax.axis_index("req")
    z = lax.axis_index("head")
    x, y, c = place(req)
    xc = x * 2 + c
    yc = y * 2 + c
    mine = (z // 2) == x
    spot = c * 8 + z

    def at_xc(i):
        return (i // 2) * 16 + y * 2 + lax.rem(i, 2)

    def dest(k):
        return (k // 4) * 16 + y * 2 + lax.rem(k // 2, 2), x * 2 + lax.rem(k, 2)

    def origin(k):
        return (z // 2) * 16 + y * 2 + k // 8, lax.rem(k, 8)

    def is_me(pair):
        return jnp.logical_and(pair[0] == req, pair[1] == z)

    def block(i, width):
        return pl.ds(pl.multiple_of(i * width, width), width)

    barrier = pltpu.get_barrier_semaphore()
    for_each(1, 64, lambda k: greet(barrier, lax.rem(req + k, 64)))

    def hello(k):
        @pl.when(jnp.logical_not(is_me(origin(k))))
        def _():
            greet(barrier, *origin(k))

    for_each(0, 16, hello)
    load = pltpu.make_async_copy(kv_ref, pages, own.at[0])
    load.start()
    own_pay = pltpu.make_async_copy(hid_ref.at[:, block(x, 128)], gathered.at[xc], own.at[1])
    own_w = pltpu.make_async_copy(w_ref.at[:, block(c, 384)], weights.at[xc], own.at[3])
    own_wo = pltpu.make_async_copy(wo_ref, wide.at[xc], own.at[2])
    own_pay.start()
    own_w.start()
    own_wo.start()

    @pl.when(mine)
    def _():
        pl.semaphore_wait(barrier, 63 + 15)

    @pl.when(jnp.logical_not(mine))
    def _():
        pl.semaphore_wait(barrier, 63 + 16)

    def send_pay(k):
        peer = lax.rem(xc + k, 8)
        return remote(
            hid_ref.at[:, block(peer // 2, 128)], gathered.at[xc], s1.at[k], r1.at[k], at_xc(peer)
        )

    def send_w(k):
        far = lax.rem(x + 1 + 2 * (k // 2), 4) * 2 + lax.rem(k, 2)
        return remote(
            w_ref.at[:, block(lax.rem(k, 2), 384)], weights.at[xc], s8.at[k], r8.at[xc], at_xc(far)
        )

    def near_w():
        return remote(
            w_ref.at[:, block(1 - c, 384)], weights.at[xc], s8.at[4], r8.at[xc],
            at_xc(x * 2 + 1 - c),
        )

    def pass_w(k):
        source = lax.rem(x + 3 + 2 * k, 4) * 2 + k
        target = lax.rem(x + 1 + 2 * k, 4) * 2 + c
        return remote(
            weights.at[source], weights.at[source], s8.at[5 + k], r8.at[source], at_xc(target)
        )

    def have_w(source):
        remote(
            weights.at[source], weights.at[source], s8.at[0], r8.at[source], at_xc(source)
        ).wait_recv()

    def send_part(k):
        peer = lax.rem(yc + k, 16)
        return remote(partial.at[peer], parts.at[yc], s2.at[k], r2.at[k], x * 16 + peer)

    def send_wo(k):
        peer = lax.rem(xc + k, 8)
        return remote(wo_ref, wide.at[xc], s3.at[k], r3.at[k], at_xc(peer))

    def ask(k):
        peer = lax.rem(req + k, 64)
        return remote(ask_buf.at[peer], asked.at[req], s4.at[k], r4.at[k], peer)

    def answer(k):
        peer = lax.rem(req - k + 64, 64)
        return remote(reply.at[peer], back.at[req], s5.at[k], r5.at[k], peer)

    def send_rows(k):
        peer = x * 16 + lax.rem(y + k, 8) * 2 + c
        return remote(heads_buf, rows.at[y], s6.at[k], r6.at[k], peer)

    def push(k):
        return remote(piece.at[k], pieces.at[spot], s7.at[k], r7.at[spot], *dest(k))

    for_each(0, 4, lambda k: send_w(k).start())
    for_each(1, 8, lambda k: send_pay(k).start())
    near_w().start()
    for k in range(2):
        have_w(lax.rem(x + 3 + 2 * k, 4) * 2 + k)
        pass_w(k).start()

    row = lax.broadcasted_iota(jnp.int32, (8, 128), 0)
    lane = lax.broadcasted_iota(jnp.int32, (8, 128), 1)
    long = jnp.zeros((8, 128), jnp.int32)
    for i in range(8):
        long = jnp.where(row == i, lengths_ref[i], long)
    table = table_ref[...]
    valid = jnp.zeros((8, 128), jnp.int32)
    for p in range(16):
        tokens = jnp.clip(long - p * 128, 0, 128)
        valid = valid + jnp.where(table[:, p : p + 1] == lane, tokens, 0)
    spread = (
        lax.broadcasted_iota(jnp.int32, (128, 512), 0) - 64
        == lax.broadcasted_iota(jnp.int32, (128, 512), 1) // 8
    )
    wanted = jnp.dot(
        valid.astype(f32).astype(bf16),
        jnp.where(spread, 1.0, 0.0).astype(bf16),
        preferred_element_type=f32,
    )
    part8 = lax.rem(lax.broadcasted_iota(jnp.int32, (8, 512), 1), 8)
    owned = [
        jnp.where(jnp.logical_and(wanted > 0.0, part8 == q), 1.0, 0.0) for q in range(4)
    ]
    asking = owned + [jnp.where(part8 >= 4, wanted, 0.0)]
    owned = jnp.concatenate(owned, axis=0)
    asking = jnp.concatenate(asking, axis=0)
    valid = jnp.concatenate([valid] * 4, axis=0)

    lane32 = lax.broadcasted_iota(jnp.int32, (32, 128), 1)

    def limit_page(e, carry):
        tokens = jnp.sum(jnp.where(lane32 == e, valid, 0), axis=1, keepdims=True)
        limits[e] = jnp.where(lane32 < tokens, 0.0, NEG_FILL)
        return carry

    lax.fori_loop(0, 64, limit_page, 0, unroll=8)
    angles = long.astype(f32) * base_ref[...]
    cosine = jnp.cos(angles)
    sine = jnp.where(lane < 64, -jnp.sin(angles), jnp.sin(angles))

    own_pay.wait()
    own_w.wait()
    for_each(1, 8, lambda k: send_pay(k).wait_recv())
    for k in range(2):
        have_w(lax.rem(x + 3 + 2 * k, 4) * 2 + 1 - k)
        have_w(lax.rem(x + 2, 4) * 2 + k)
    have_w(x * 2 + 1 - c)
    for_each(1, 8, lambda k: send_wo(k).start())
    sums = dot_tn(gathered[...].reshape(512, 128), weights[...].reshape(512, 384))
    partial[...] = sums.reshape(16, 8, 384).astype(bf16)
    own_part = pltpu.make_async_copy(partial.at[yc], parts.at[yc], own.at[1])
    own_part.start()
    for_each(1, 16, lambda k: send_part(k).start())
    own_part.wait()
    for_each(1, 16, lambda k: send_part(k).wait_recv())
    total = parts[0:2].astype(f32)
    for i in range(1, 8):
        total = total + parts[2 * i : 2 * i + 2].astype(f32)
    made = [total[h // 3, :, 128 * (h % 3) : 128 * (h % 3) + 128] for h in range(6)]

    def turn(v):
        return (v * cosine + pltpu.roll(v, 64, 1) * sine).astype(bf16).astype(f32)

    queries = jnp.concatenate([turn(made[q]) for q in range(4)], axis=0)
    new_keys = jnp.concatenate([turn(made[4])] * 4, axis=0)
    new_values = jnp.concatenate([made[5].astype(bf16).astype(f32)] * 4, axis=0)
    self_scores = jnp.sum(queries * new_keys, axis=1, keepdims=True) * SCALE
    ask_rows = dot_tn(
        asking.astype(bf16),
        jnp.concatenate([queries, jnp.ones((8, 128), f32)], axis=0).astype(bf16),
    )
    ask_buf[...] = ask_rows.reshape(64, 8, 128).astype(bf16)
    own_ask = pltpu.make_async_copy(ask_buf.at[req], asked.at[req], own.at[1])
    own_ask.start()
    for_each(1, 64, lambda k: ask(k).start())
    load.wait()

    queries = queries.astype(bf16)

    def score(e, top):
        s = dot_nt(queries, pages[e, :, 0:128]) * SCALE
        s = jnp.where(limits[e] == 0.0, s, NEG_FILL)
        scores[e] = s
        return jnp.maximum(top, s)

    near_max = lax.fori_loop(0, 64, score, jnp.full((32, 128), NEG_FILL, f32), unroll=8)
    near_max = jnp.max(near_max, axis=1, keepdims=True)

    def gather(e, carry):
        acc, weight = carry
        s = scores[e]
        w = jnp.where(s > 0.5 * NEG_FILL, jnp.exp(s - near_max), 0.0)
        return acc + jnp.dot(w.astype(bf16), pages[e, :, 128:256], preferred_element_type=f32), weight + w

    zero = jnp.zeros((32, 128), f32)
    near, near_sum = lax.fori_loop(0, 64, gather, (zero, zero), unroll=8)
    near_sum = jnp.sum(near_sum, axis=1, keepdims=True)

    own_ask.wait()
    batch = 16
    row3 = lax.broadcasted_iota(jnp.int32, (batch, 8, 128), 1)
    lane3 = lax.broadcasted_iota(jnp.int32, (batch, 8, 128), 2)
    own_answer = pltpu.make_async_copy(reply.at[req], back.at[req], own.at[0])

    def serve(j, carry):
        first = j * batch

        def heard(k):
            @pl.when(k > 0)
            def _():
                ask(k).wait_recv()

        def tell(k):
            @pl.when(k > 0)
            def _():
                answer(k).start()

        for_each(first, first + batch, heard)
        sources = [lax.rem(req - first - i + 64, 64) for i in range(batch)]
        slots = [slots_ref[g] for g in sources]
        query, limit = [], []
        for g in sources:
            both = asked[g].astype(f32)
            other = pltpu.roll(both, 4, 0)
            query.append(jnp.where(row < 4, both, other).astype(bf16))
            limit.append(jnp.where(row < 4, other, both))
        limit = jnp.stack(limit)
        s = jnp.stack([dot_nt(query[i], pages[slots[i], :, 0:128]) for i in range(batch)]) * SCALE
        mask = lane3.astype(f32) < limit
        s = jnp.where(mask, s, NEG_FILL)
        m = jnp.max(s, axis=2, keepdims=True)
        w = jnp.where(mask, jnp.exp(s - m), 0.0)
        l = jnp.sum(w, axis=2, keepdims=True)
        m0, m1, m2 = split_three(jnp.broadcast_to(m, s.shape))
        l0, l1, l2 = split_three(jnp.broadcast_to(l, s.shape))
        stats = jnp.where(lane3 < 16, m0, jnp.where(lane3 < 32, m1, jnp.where(lane3 < 48, m2,
                jnp.where(lane3 < 64, l0, jnp.where(lane3 < 80, l1, l2)))))
        for i in range(batch):
            a = jnp.dot(
                w[i].astype(bf16), pages[slots[i], :, 128:256], preferred_element_type=f32
            )
            reply[sources[i]] = jnp.where(row < 4, a, stats[i]).astype(bf16)
        for_each(first, first + batch, tell)
        return carry

    lax.fori_loop(0, 64 // batch, serve, 0)
    own_answer.start()
    own_answer.wait()
    for_each(1, 64, lambda k: answer(k).wait_recv())

    far = back[...].astype(f32).reshape(512, 128).astype(bf16)
    pick_max = jnp.logical_and(lane < 48, lax.rem(lane, 16) == 0)
    pick_sum = jnp.logical_and(
        jnp.logical_and(lane >= 48, lane < 96), lax.rem(lane, 16) == 0
    )
    far_max = dot_nt(jnp.where(pick_max, 1.0, 0.0).astype(bf16), far)
    far_sum = dot_nt(jnp.where(pick_sum, 1.0, 0.0).astype(bf16), far)
    far_max = jnp.concatenate([pltpu.roll(far_max, 508, 1)] * 4, axis=0)
    far_sum = jnp.concatenate([pltpu.roll(far_sum, 508, 1)] * 4, axis=0)
    picked = owned > 0.5
    peak = jnp.max(jnp.where(picked, far_max, NEG_FILL), axis=1, keepdims=True)
    peak = jnp.maximum(jnp.maximum(peak, near_max), self_scores)
    factors = jnp.where(picked, jnp.exp(jnp.minimum(far_max - peak, 0.0)), 0.0)
    near_factor = jnp.exp(near_max - peak)
    self_factor = jnp.exp(self_scores - peak)
    weight_sum = (
        jnp.sum(jnp.where(picked, factors * far_sum, 0.0), axis=1, keepdims=True)
        + near_factor * near_sum + self_factor
    )
    high = factors.astype(bf16)
    low = (factors - high.astype(f32)).astype(bf16)
    weighted = (
        jnp.dot(high, far, preferred_element_type=f32)
        + jnp.dot(low, far, preferred_element_type=f32)
        + near_factor * near + self_factor * new_values
    )
    heads_buf[...] = (weighted / weight_sum).astype(bf16)

    own_rows = pltpu.make_async_copy(heads_buf, rows.at[y], own.at[0])
    own_rows.start()
    for_each(1, 8, lambda k: send_rows(k).start())
    own_wo.wait()
    for_each(1, 8, lambda k: send_wo(k).wait_recv())
    own_rows.wait()
    for_each(1, 8, lambda k: send_rows(k).wait_recv())
    heads = rows[...].astype(f32)
    heads = jnp.concatenate(
        [heads[:, 8 * q : 8 * q + 8].reshape(64, 128) for q in range(4)], axis=1
    ).astype(bf16)
    for i in range(8):
        tile = dot_nt(heads, wide[i]).astype(bf16)
        piece[2 * i] = tile[0:32]
        piece[2 * i + 1] = tile[32:64]

    def send(k):
        @pl.when(is_me(dest(k)))
        def _():
            pltpu.make_async_copy(piece.at[k], pieces.at[spot], r7.at[spot]).start()

        @pl.when(jnp.logical_not(is_me(dest(k))))
        def _():
            push(k).start()

    for_each(0, 16, send)
    for_each(1, 64, lambda k: ask(k).wait_send())
    for_each(1, 64, lambda k: answer(k).wait_send())
    for_each(1, 8, lambda k: send_pay(k).wait_send())
    for_each(0, 4, lambda k: send_w(k).wait_send())
    near_w().wait_send()
    for k in range(2):
        pass_w(k).wait_send()
    for_each(1, 16, lambda k: send_part(k).wait_send())
    for_each(1, 8, lambda k: send_wo(k).wait_send())
    for_each(1, 8, lambda k: send_rows(k).wait_send())

    def receive(k):
        pltpu.make_async_copy(pieces.at[k], pieces.at[k], r7.at[k]).wait()

    for_each(0, 16, receive)
    totals = []
    for j in range(2):
        total = pieces[8 * j].astype(f32)
        for h in range(1, 8):
            total = total + pieces[8 * j + h].astype(f32)
        totals.append(total)
    out_ref[...] = jnp.concatenate(
        [totals[j][8 * i : 8 * i + 8] for i in range(4) for j in range(2)], axis=0
    ).astype(bf16)

    def sent(k):
        @pl.when(jnp.logical_not(is_me(dest(k))))
        def _():
            push(k).wait_send()

    for_each(0, 16, sent)


def vmem():
    return pl.BlockSpec(memory_space=pltpu.VMEM)


def params(ident):
    return pltpu.CompilerParams(collective_id=ident, has_side_effects=True)


def dma(count):
    return pltpu.SemaphoreType.DMA((count,))


def shards(hidden, query_key_value_weight, output_weight, kv_pool, lengths, page_table, send_slots):
    bf16, f32 = jnp.bfloat16, jnp.float32
    exponent = np.arange(128) % 64 * (2.0 / 128)
    base = np.broadcast_to(ROPE_BASE ** -exponent, (8, 128)).astype(np.float32)
    smem = pl.BlockSpec(memory_space=pltpu.SMEM)
    return pl.pallas_call(
        layer_kernel,
        out_shape=jax.ShapeDtypeStruct((64, 64), bf16),
        in_specs=[smem, smem] + [vmem()] * 5 + [pl.BlockSpec(memory_space=pl.ANY)],
        out_specs=vmem(),
        scratch_shapes=[
            pltpu.VMEM((8, 64, 128), bf16),
            pltpu.VMEM((8, 64, 384), bf16),
            pltpu.VMEM((8, 64, 512), bf16),
            pltpu.VMEM((16, 8, 384), bf16),
            pltpu.VMEM((16, 8, 384), bf16),
            pltpu.VMEM((64, 128, 256), bf16),
            pltpu.VMEM((64, 32, 128), f32),
            pltpu.VMEM((64, 8, 128), bf16),
            pltpu.VMEM((64, 8, 128), bf16),
            pltpu.VMEM((64, 32, 128), f32),
            pltpu.VMEM((64, 8, 128), bf16),
            pltpu.VMEM((64, 8, 128), bf16),
            pltpu.VMEM((32, 128), bf16),
            pltpu.VMEM((8, 32, 128), bf16),
            pltpu.VMEM((16, 32, 64), bf16),
            pltpu.VMEM((16, 32, 64), bf16),
            dma(4), dma(8), dma(8), dma(16), dma(16), dma(8), dma(8), dma(64), dma(64),
            dma(64), dma(64), dma(8), dma(8), dma(16), dma(16),
            dma(7), dma(8),
        ],
        compiler_params=params(1),
    )(
        send_slots, lengths, page_table, jnp.asarray(base),
        hidden.T, query_key_value_weight.reshape(64, 768), output_weight.T, kv_pool.reshape(64, 128, 256),
    )


def solution(mesh):
    return jax.shard_map(
        shards,
        mesh=mesh,
        in_specs=(
            P(None, "req"),
            P("req", "head", None),
            P("head", "req"),
            P("req", "head", None, None),
            P("req"),
            P("req", None),
            P("req"),
        ),
        out_specs=P("head", "req"),
        check_vma=False,
    )
```

```python
import jax
import jax.numpy as jnp
import numpy as np
from jax import lax
from jax.experimental import pallas as pl
from jax.experimental.pallas import tpu as pltpu
from jax.sharding import PartitionSpec as P

ROPE_BASE = 500000.0
NEG_FILL = -1e30
SCALE = 128 ** (-0.5)


def remote(src, dst, send, recv, req, head=None):
    where = {"req": req} if head is None else {"req": req, "head": head}
    return pltpu.make_async_remote_copy(
        src_ref=src, dst_ref=dst, send_sem=send, recv_sem=recv,
        device_id=where, device_id_type=pl.DeviceIdType.MESH,
    )


def greet(barrier, req, head=None):
    where = {"req": req} if head is None else {"req": req, "head": head}
    pl.semaphore_signal(barrier, inc=1, device_id=where, device_id_type=pl.DeviceIdType.MESH)


def for_each(start, stop, body):
    def step(i, carry):
        body(i)
        return carry
    lax.fori_loop(start, stop, step, 0)


def place(req):
    return req // 16, lax.rem(req // 2, 8), lax.rem(req, 2)


def split_three(v):
    high = v.astype(jnp.bfloat16).astype(jnp.float32)
    rest = v - high
    mid = rest.astype(jnp.bfloat16).astype(jnp.float32)
    return high, mid, rest - mid


def dot_nt(a, b):
    return lax.dot_general(a, b, (((1,), (1,)), ((), ())), preferred_element_type=jnp.float32)


def dot_tn(a, b):
    return lax.dot_general(a, b, (((0,), (0,)), ((), ())), preferred_element_type=jnp.float32)


def layer_kernel(
    slots_ref, lengths_ref, table_ref, base_ref, hid_ref, w_ref, wo_ref, kv_ref, out_ref,
    gathered, weights, wide, partial, parts, pages, limits, ask_buf, asked, scores, reply, back, heads_buf, rows,
    piece, pieces, own, s1, r1, s2, r2, s3, r3, s4, r4, s5, r5, s6, r6, s7, r7,
    s8, r8,
):
    bf16, f32 = jnp.bfloat16, jnp.float32
    req = lax.axis_index("req")
    z = lax.axis_index("head")
    x, y, c = place(req)
    xc = x * 2 + c
    yc = y * 2 + c
    mine = (z // 2) == x
    spot = c * 8 + z

    def at_xc(i):
        return (i // 2) * 16 + y * 2 + lax.rem(i, 2)

    def dest(k):
        return (k // 4) * 16 + y * 2 + lax.rem(k // 2, 2), x * 2 + lax.rem(k, 2)

    def origin(k):
        return (z // 2) * 16 + y * 2 + k // 8, lax.rem(k, 8)

    def is_me(pair):
        return jnp.logical_and(pair[0] == req, pair[1] == z)

    def block(i, width):
        return pl.ds(pl.multiple_of(i * width, width), width)

    barrier = pltpu.get_barrier_semaphore()
    for_each(1, 64, lambda k: greet(barrier, lax.rem(req + k, 64)))

    def hello(k):
        @pl.when(jnp.logical_not(is_me(origin(k))))
        def _():
            greet(barrier, *origin(k))

    for_each(0, 16, hello)
    load = pltpu.make_async_copy(kv_ref, pages, own.at[0])
    load.start()
    own_pay = pltpu.make_async_copy(hid_ref.at[:, block(x, 128)], gathered.at[xc], own.at[1])
    own_w = pltpu.make_async_copy(w_ref.at[:, block(c, 384)], weights.at[xc], own.at[3])
    own_wo = pltpu.make_async_copy(wo_ref, wide.at[xc], own.at[2])
    own_pay.start()
    own_w.start()
    own_wo.start()

    @pl.when(mine)
    def _():
        pl.semaphore_wait(barrier, 63 + 15)

    @pl.when(jnp.logical_not(mine))
    def _():
        pl.semaphore_wait(barrier, 63 + 16)

    def send_pay(k):
        peer = lax.rem(xc + k, 8)
        return remote(
            hid_ref.at[:, block(peer // 2, 128)], gathered.at[xc], s1.at[k], r1.at[k], at_xc(peer)
        )

    def send_w(k):
        far = lax.rem(x + 1 + 2 * (k // 2), 4) * 2 + lax.rem(k, 2)
        return remote(
            w_ref.at[:, block(lax.rem(k, 2), 384)], weights.at[xc], s8.at[k], r8.at[xc], at_xc(far)
        )

    def near_w():
        return remote(
            w_ref.at[:, block(1 - c, 384)], weights.at[xc], s8.at[4], r8.at[xc],
            at_xc(x * 2 + 1 - c),
        )

    def pass_w(k):
        source = lax.rem(x + 3 + 2 * k, 4) * 2 + k
        target = lax.rem(x + 1 + 2 * k, 4) * 2 + c
        return remote(
            weights.at[source], weights.at[source], s8.at[5 + k], r8.at[source], at_xc(target)
        )

    def have_w(source):
        remote(
            weights.at[source], weights.at[source], s8.at[0], r8.at[source], at_xc(source)
        ).wait_recv()

    def send_part(k):
        peer = lax.rem(yc + k, 16)
        return remote(partial.at[peer], parts.at[yc], s2.at[k], r2.at[k], x * 16 + peer)

    def send_wo(k):
        peer = lax.rem(xc + k, 8)
        return remote(wo_ref, wide.at[xc], s3.at[k], r3.at[k], at_xc(peer))

    def ask(k):
        peer = lax.rem(req + k, 64)
        return remote(ask_buf.at[peer], asked.at[req], s4.at[k], r4.at[k], peer)

    def answer(k):
        peer = lax.rem(req - k + 64, 64)
        return remote(reply.at[peer], back.at[req], s5.at[k], r5.at[k], peer)

    def send_rows(k):
        peer = x * 16 + lax.rem(y + k, 8) * 2 + c
        return remote(heads_buf, rows.at[y], s6.at[k], r6.at[k], peer)

    def push(k):
        return remote(piece.at[k], pieces.at[spot], s7.at[k], r7.at[spot], *dest(k))

    for_each(0, 4, lambda k: send_w(k).start())
    for_each(1, 8, lambda k: send_pay(k).start())
    near_w().start()
    for k in range(2):
        have_w(lax.rem(x + 3 + 2 * k, 4) * 2 + k)
        pass_w(k).start()

    row = lax.broadcasted_iota(jnp.int32, (8, 128), 0)
    lane = lax.broadcasted_iota(jnp.int32, (8, 128), 1)
    long = jnp.zeros((8, 128), jnp.int32)
    for i in range(8):
        long = jnp.where(row == i, lengths_ref[i], long)
    table = table_ref[...]
    valid = jnp.zeros((8, 128), jnp.int32)
    for p in range(16):
        tokens = jnp.clip(long - p * 128, 0, 128)
        valid = valid + jnp.where(table[:, p : p + 1] == lane, tokens, 0)
    spread = (
        lax.broadcasted_iota(jnp.int32, (128, 512), 0) - 64
        == lax.broadcasted_iota(jnp.int32, (128, 512), 1) // 8
    )
    wanted = jnp.dot(
        valid.astype(f32).astype(bf16),
        jnp.where(spread, 1.0, 0.0).astype(bf16),
        preferred_element_type=f32,
    )
    part8 = lax.rem(lax.broadcasted_iota(jnp.int32, (8, 512), 1), 8)
    owned = [
        jnp.where(jnp.logical_and(wanted > 0.0, part8 == q), 1.0, 0.0) for q in range(4)
    ]
    asking = owned + [jnp.where(part8 >= 4, wanted, 0.0)]
    owned = jnp.concatenate(owned, axis=0)
    asking = jnp.concatenate(asking, axis=0)
    valid = jnp.concatenate([valid] * 4, axis=0)

    angles = long.astype(f32) * base_ref[...]
    cosine = jnp.cos(angles)
    sine = jnp.where(lane < 64, -jnp.sin(angles), jnp.sin(angles))

    own_pay.wait()
    own_w.wait()
    for_each(1, 8, lambda k: send_pay(k).wait_recv())
    for k in range(2):
        have_w(lax.rem(x + 3 + 2 * k, 4) * 2 + 1 - k)
        have_w(lax.rem(x + 2, 4) * 2 + k)
    have_w(x * 2 + 1 - c)
    sums = dot_tn(gathered[...].reshape(512, 128), weights[...].reshape(512, 384))
    partial[...] = sums.reshape(16, 8, 384).astype(bf16)
    own_part = pltpu.make_async_copy(partial.at[yc], parts.at[yc], own.at[1])
    own_part.start()
    for_each(1, 16, lambda k: send_part(k).start())
    lane32 = lax.broadcasted_iota(jnp.int32, (32, 128), 1)

    def limit_page(e, carry):
        tokens = jnp.sum(jnp.where(lane32 == e, valid, 0), axis=1, keepdims=True)
        limits[e] = jnp.where(lane32 < tokens, 0.0, NEG_FILL)
        return carry

    lax.fori_loop(0, 64, limit_page, 0, unroll=8)
    own_part.wait()
    for_each(1, 16, lambda k: send_part(k).wait_recv())
    total = parts[0:2].astype(f32)
    for i in range(1, 8):
        total = total + parts[2 * i : 2 * i + 2].astype(f32)
    made = [total[h // 3, :, 128 * (h % 3) : 128 * (h % 3) + 128] for h in range(6)]

    def turn(v):
        return (v * cosine + pltpu.roll(v, 64, 1) * sine).astype(bf16).astype(f32)

    queries = jnp.concatenate([turn(made[q]) for q in range(4)], axis=0)
    new_keys = jnp.concatenate([turn(made[4])] * 4, axis=0)
    new_values = jnp.concatenate([made[5].astype(bf16).astype(f32)] * 4, axis=0)
    self_scores = jnp.sum(queries * new_keys, axis=1, keepdims=True) * SCALE
    ask_rows = dot_tn(
        asking.astype(bf16),
        jnp.concatenate([queries, jnp.ones((8, 128), f32)], axis=0).astype(bf16),
    )
    ask_buf[...] = ask_rows.reshape(64, 8, 128).astype(bf16)
    own_ask = pltpu.make_async_copy(ask_buf.at[req], asked.at[req], own.at[1])
    own_ask.start()
    for_each(1, 64, lambda k: ask(k).start())
    load.wait()

    queries = queries.astype(bf16)

    def score(e, top):
        s = dot_nt(queries, pages[e, :, 0:128]) * SCALE
        s = jnp.where(limits[e] == 0.0, s, NEG_FILL)
        scores[e] = s
        return jnp.maximum(top, s)

    near_max = lax.fori_loop(0, 64, score, jnp.full((32, 128), NEG_FILL, f32), unroll=8)
    near_max = jnp.max(near_max, axis=1, keepdims=True)

    own_ask.wait()
    batch = 16
    row3 = lax.broadcasted_iota(jnp.int32, (batch, 8, 128), 1)
    lane3 = lax.broadcasted_iota(jnp.int32, (batch, 8, 128), 2)
    own_answer = pltpu.make_async_copy(reply.at[req], back.at[req], own.at[0])

    def serve(j, carry):
        first = j * batch

        def heard(k):
            @pl.when(k > 0)
            def _():
                ask(k).wait_recv()

        def tell(k):
            @pl.when(k > 0)
            def _():
                answer(k).start()

        for_each(first, first + batch, heard)
        sources = [lax.rem(req - first - i + 64, 64) for i in range(batch)]
        slots = [slots_ref[g] for g in sources]
        query, limit = [], []
        for g in sources:
            both = asked[g].astype(f32)
            other = pltpu.roll(both, 4, 0)
            query.append(jnp.where(row < 4, both, other).astype(bf16))
            limit.append(jnp.where(row < 4, other, both))
        limit = jnp.stack(limit)
        s = jnp.stack([dot_nt(query[i], pages[slots[i], :, 0:128]) for i in range(batch)]) * SCALE
        mask = lane3.astype(f32) < limit
        s = jnp.where(mask, s, NEG_FILL)
        m = jnp.max(s, axis=2, keepdims=True)
        w = jnp.where(mask, jnp.exp(s - m), 0.0)
        l = jnp.sum(w, axis=2, keepdims=True)
        m0, m1, m2 = split_three(jnp.broadcast_to(m, s.shape))
        l0, l1, l2 = split_three(jnp.broadcast_to(l, s.shape))
        stats = jnp.where(lane3 < 16, m0, jnp.where(lane3 < 32, m1, jnp.where(lane3 < 48, m2,
                jnp.where(lane3 < 64, l0, jnp.where(lane3 < 80, l1, l2)))))
        for i in range(batch):
            a = jnp.dot(
                w[i].astype(bf16), pages[slots[i], :, 128:256], preferred_element_type=f32
            )
            reply[sources[i]] = jnp.where(row < 4, a, stats[i]).astype(bf16)
        for_each(first, first + batch, tell)
        return carry

    lax.fori_loop(0, 64 // batch, serve, 0)
    own_answer.start()
    for_each(1, 8, lambda k: send_wo(k).start())
    def gather(e, carry):
        acc, weight = carry
        s = scores[e]
        w = jnp.where(s > 0.5 * NEG_FILL, jnp.exp(s - near_max), 0.0)
        return acc + jnp.dot(w.astype(bf16), pages[e, :, 128:256], preferred_element_type=f32), weight + w

    zero = jnp.zeros((32, 128), f32)
    near, near_sum = lax.fori_loop(0, 64, gather, (zero, zero), unroll=8)
    near_sum = jnp.sum(near_sum, axis=1, keepdims=True)

    own_answer.wait()
    for_each(1, 64, lambda k: answer(k).wait_recv())

    far = back[...].astype(f32).reshape(512, 128).astype(bf16)
    pick_max = jnp.logical_and(lane < 48, lax.rem(lane, 16) == 0)
    pick_sum = jnp.logical_and(
        jnp.logical_and(lane >= 48, lane < 96), lax.rem(lane, 16) == 0
    )
    far_max = dot_nt(jnp.where(pick_max, 1.0, 0.0).astype(bf16), far)
    far_sum = dot_nt(jnp.where(pick_sum, 1.0, 0.0).astype(bf16), far)
    far_max = jnp.concatenate([pltpu.roll(far_max, 508, 1)] * 4, axis=0)
    far_sum = jnp.concatenate([pltpu.roll(far_sum, 508, 1)] * 4, axis=0)
    picked = owned > 0.5
    peak = jnp.max(jnp.where(picked, far_max, NEG_FILL), axis=1, keepdims=True)
    peak = jnp.maximum(jnp.maximum(peak, near_max), self_scores)
    factors = jnp.where(picked, jnp.exp(jnp.minimum(far_max - peak, 0.0)), 0.0)
    near_factor = jnp.exp(near_max - peak)
    self_factor = jnp.exp(self_scores - peak)
    weight_sum = (
        jnp.sum(jnp.where(picked, factors * far_sum, 0.0), axis=1, keepdims=True)
        + near_factor * near_sum + self_factor
    )
    high = factors.astype(bf16)
    low = (factors - high.astype(f32)).astype(bf16)
    weighted = (
        jnp.dot(high, far, preferred_element_type=f32)
        + jnp.dot(low, far, preferred_element_type=f32)
        + near_factor * near + self_factor * new_values
    )
    heads_buf[...] = (weighted / weight_sum).astype(bf16)

    own_rows = pltpu.make_async_copy(heads_buf, rows.at[y], own.at[0])
    own_rows.start()
    for_each(1, 8, lambda k: send_rows(k).start())
    own_wo.wait()
    for_each(1, 8, lambda k: send_wo(k).wait_recv())
    own_rows.wait()
    for_each(1, 8, lambda k: send_rows(k).wait_recv())
    heads = rows[...].astype(f32)
    heads = jnp.concatenate(
        [heads[:, 8 * q : 8 * q + 8].reshape(64, 128) for q in range(4)], axis=1
    ).astype(bf16)
    for i in range(8):
        tile = dot_nt(heads, wide[i]).astype(bf16)
        piece[2 * i] = tile[0:32]
        piece[2 * i + 1] = tile[32:64]

    def send(k):
        @pl.when(is_me(dest(k)))
        def _():
            pltpu.make_async_copy(piece.at[k], pieces.at[spot], r7.at[spot]).start()

        @pl.when(jnp.logical_not(is_me(dest(k))))
        def _():
            push(k).start()

    for_each(0, 16, send)
    for_each(1, 64, lambda k: ask(k).wait_send())
    for_each(1, 64, lambda k: answer(k).wait_send())
    for_each(1, 8, lambda k: send_pay(k).wait_send())
    for_each(0, 4, lambda k: send_w(k).wait_send())
    near_w().wait_send()
    for k in range(2):
        pass_w(k).wait_send()
    for_each(1, 16, lambda k: send_part(k).wait_send())
    for_each(1, 8, lambda k: send_wo(k).wait_send())
    for_each(1, 8, lambda k: send_rows(k).wait_send())

    def receive(k):
        pltpu.make_async_copy(pieces.at[k], pieces.at[k], r7.at[k]).wait()

    for_each(0, 16, receive)
    totals = []
    for j in range(2):
        total = pieces[8 * j].astype(f32)
        for h in range(1, 8):
            total = total + pieces[8 * j + h].astype(f32)
        totals.append(total)
    out_ref[...] = jnp.concatenate(
        [totals[j][8 * i : 8 * i + 8] for i in range(4) for j in range(2)], axis=0
    ).astype(bf16)

    def sent(k):
        @pl.when(jnp.logical_not(is_me(dest(k))))
        def _():
            push(k).wait_send()

    for_each(0, 16, sent)


def vmem():
    return pl.BlockSpec(memory_space=pltpu.VMEM)


def params(ident):
    return pltpu.CompilerParams(collective_id=ident, has_side_effects=True)


def dma(count):
    return pltpu.SemaphoreType.DMA((count,))


def shards(hidden, query_key_value_weight, output_weight, kv_pool, lengths, page_table, send_slots):
    bf16, f32 = jnp.bfloat16, jnp.float32
    exponent = np.arange(128) % 64 * (2.0 / 128)
    base = np.broadcast_to(ROPE_BASE ** -exponent, (8, 128)).astype(np.float32)
    smem = pl.BlockSpec(memory_space=pltpu.SMEM)
    return pl.pallas_call(
        layer_kernel,
        out_shape=jax.ShapeDtypeStruct((64, 64), bf16),
        in_specs=[smem, smem] + [vmem()] * 5 + [pl.BlockSpec(memory_space=pl.ANY)],
        out_specs=vmem(),
        scratch_shapes=[
            pltpu.VMEM((8, 64, 128), bf16),
            pltpu.VMEM((8, 64, 384), bf16),
            pltpu.VMEM((8, 64, 512), bf16),
            pltpu.VMEM((16, 8, 384), bf16),
            pltpu.VMEM((16, 8, 384), bf16),
            pltpu.VMEM((64, 128, 256), bf16),
            pltpu.VMEM((64, 32, 128), f32),
            pltpu.VMEM((64, 8, 128), bf16),
            pltpu.VMEM((64, 8, 128), bf16),
            pltpu.VMEM((64, 32, 128), f32),
            pltpu.VMEM((64, 8, 128), bf16),
            pltpu.VMEM((64, 8, 128), bf16),
            pltpu.VMEM((32, 128), bf16),
            pltpu.VMEM((8, 32, 128), bf16),
            pltpu.VMEM((16, 32, 64), bf16),
            pltpu.VMEM((16, 32, 64), bf16),
            dma(4), dma(8), dma(8), dma(16), dma(16), dma(8), dma(8), dma(64), dma(64),
            dma(64), dma(64), dma(8), dma(8), dma(16), dma(16),
            dma(7), dma(8),
        ],
        compiler_params=params(1),
    )(
        send_slots, lengths, page_table, jnp.asarray(base),
        hidden.T, query_key_value_weight.reshape(64, 768), output_weight.T, kv_pool.reshape(64, 128, 256),
    )


def solution(mesh):
    return jax.shard_map(
        shards,
        mesh=mesh,
        in_specs=(
            P(None, "req"),
            P("req", "head", None),
            P("head", "req"),
            P("req", "head", None, None),
            P("req"),
            P("req", None),
            P("req"),
        ),
        out_specs=P("head", "req"),
        check_vma=False,
    )
```

```python
import jax
import jax.numpy as jnp
import numpy as np
from jax import lax
from jax.experimental import pallas as pl
from jax.experimental.pallas import tpu as pltpu
from jax.sharding import PartitionSpec as P

ROPE_BASE = 500000.0
NEG_FILL = -1e30
SCALE = 128 ** (-0.5)


def remote(src, dst, send, recv, req, head=None):
    where = {"req": req} if head is None else {"req": req, "head": head}
    return pltpu.make_async_remote_copy(
        src_ref=src, dst_ref=dst, send_sem=send, recv_sem=recv,
        device_id=where, device_id_type=pl.DeviceIdType.MESH,
    )


def greet(barrier, req, head=None):
    where = {"req": req} if head is None else {"req": req, "head": head}
    pl.semaphore_signal(barrier, inc=1, device_id=where, device_id_type=pl.DeviceIdType.MESH)


def for_each(start, stop, body):
    def step(i, carry):
        body(i)
        return carry
    unroll = {63: 7, 15: 5, 16: 4, 7: 7, 4: 4}.get(stop - start, 1)
    lax.fori_loop(start, stop, step, 0, unroll=unroll)


def place(req):
    return req // 16, lax.rem(req // 2, 8), lax.rem(req, 2)


def split_three(v):
    high = v.astype(jnp.bfloat16).astype(jnp.float32)
    rest = v - high
    mid = rest.astype(jnp.bfloat16).astype(jnp.float32)
    return high, mid, rest - mid


def dot_nt(a, b):
    return lax.dot_general(a, b, (((1,), (1,)), ((), ())), preferred_element_type=jnp.float32)


def dot_tn(a, b):
    return lax.dot_general(a, b, (((0,), (0,)), ((), ())), preferred_element_type=jnp.float32)


def layer_kernel(
    slots_ref, lengths_ref, table_ref, base_ref, hid_ref, w_ref, wo_ref, kv_ref, out_ref,
    gathered, weights, wide, partial, parts, pages, limits, ask_buf, asked, scores, reply, back, heads_buf, rows,
    piece, pieces, own, s1, r1, s2, r2, s3, r3, s4, r4, s5, r5, s6, r6, s7, r7,
    s8, r8,
):
    bf16, f32 = jnp.bfloat16, jnp.float32
    req = lax.axis_index("req")
    z = lax.axis_index("head")
    x, y, c = place(req)
    xc = x * 2 + c
    yc = y * 2 + c
    mine = (z // 2) == x
    spot = c * 8 + z

    def at_xc(i):
        return (i // 2) * 16 + y * 2 + lax.rem(i, 2)

    def dest(k):
        return (k // 4) * 16 + y * 2 + lax.rem(k // 2, 2), x * 2 + lax.rem(k, 2)

    def origin(k):
        return (z // 2) * 16 + y * 2 + k // 8, lax.rem(k, 8)

    def is_me(pair):
        return jnp.logical_and(pair[0] == req, pair[1] == z)

    def block(i, width):
        return pl.ds(pl.multiple_of(i * width, width), width)

    barrier = pltpu.get_barrier_semaphore()
    for_each(1, 64, lambda k: greet(barrier, lax.rem(req + k, 64)))

    def hello(k):
        @pl.when(jnp.logical_not(is_me(origin(k))))
        def _():
            greet(barrier, *origin(k))

    for_each(0, 16, hello)
    load = pltpu.make_async_copy(kv_ref, pages, own.at[0])
    load.start()
    own_pay = pltpu.make_async_copy(hid_ref.at[:, block(x, 128)], gathered.at[xc], own.at[1])
    own_w = pltpu.make_async_copy(w_ref.at[:, block(c, 384)], weights.at[xc], own.at[3])
    own_wo = pltpu.make_async_copy(wo_ref, wide.at[xc], own.at[2])
    own_pay.start()
    own_w.start()
    own_wo.start()

    @pl.when(mine)
    def _():
        pl.semaphore_wait(barrier, 63 + 15)

    @pl.when(jnp.logical_not(mine))
    def _():
        pl.semaphore_wait(barrier, 63 + 16)

    def send_pay(k):
        peer = lax.rem(xc + k, 8)
        return remote(
            hid_ref.at[:, block(peer // 2, 128)], gathered.at[xc], s1.at[k], r1.at[k], at_xc(peer)
        )

    def send_w(k):
        far = lax.rem(x + 1 + 2 * (k // 2), 4) * 2 + lax.rem(k, 2)
        return remote(
            w_ref.at[:, block(lax.rem(k, 2), 384)], weights.at[xc], s8.at[k], r8.at[xc], at_xc(far)
        )

    def near_w():
        return remote(
            w_ref.at[:, block(1 - c, 384)], weights.at[xc], s8.at[4], r8.at[xc],
            at_xc(x * 2 + 1 - c),
        )

    def pass_w(k):
        source = lax.rem(x + 3 + 2 * k, 4) * 2 + k
        target = lax.rem(x + 1 + 2 * k, 4) * 2 + c
        return remote(
            weights.at[source], weights.at[source], s8.at[5 + k], r8.at[source], at_xc(target)
        )

    def have_w(source):
        remote(
            weights.at[source], weights.at[source], s8.at[0], r8.at[source], at_xc(source)
        ).wait_recv()

    def send_part(k):
        peer = lax.rem(yc + k, 16)
        return remote(partial.at[peer], parts.at[yc], s2.at[k], r2.at[k], x * 16 + peer)

    def send_wo(k):
        peer = lax.rem(xc + k, 8)
        return remote(wo_ref, wide.at[xc], s3.at[k], r3.at[k], at_xc(peer))

    def ask(k):
        peer = lax.rem(req + k, 64)
        return remote(ask_buf.at[peer], asked.at[req], s4.at[k], r4.at[k], peer)

    def answer(k):
        peer = lax.rem(req - k + 64, 64)
        return remote(reply.at[peer], back.at[req], s5.at[k], r5.at[0], peer)

    def send_rows(k):
        peer = x * 16 + lax.rem(y + k, 8) * 2 + c
        return remote(heads_buf, rows.at[y], s6.at[k], r6.at[k], peer)

    def push(k):
        return remote(piece.at[k], pieces.at[spot], s7.at[k], r7.at[spot], *dest(k))

    for_each(0, 4, lambda k: send_w(k).start())
    for_each(1, 8, lambda k: send_pay(k).start())
    near_w().start()
    for k in range(2):
        have_w(lax.rem(x + 3 + 2 * k, 4) * 2 + k)
        pass_w(k).start()

    row = lax.broadcasted_iota(jnp.int32, (8, 128), 0)
    lane = lax.broadcasted_iota(jnp.int32, (8, 128), 1)
    long = jnp.zeros((8, 128), jnp.int32)
    for i in range(8):
        long = jnp.where(row == i, lengths_ref[i], long)
    table = table_ref[...]
    valid = jnp.zeros((8, 128), jnp.int32)
    for p in range(16):
        tokens = jnp.clip(long - p * 128, 0, 128)
        valid = valid + jnp.where(table[:, p : p + 1] == lane, tokens, 0)
    spread = (
        lax.broadcasted_iota(jnp.int32, (128, 512), 0) - 64
        == lax.broadcasted_iota(jnp.int32, (128, 512), 1) // 8
    )
    wanted = jnp.dot(
        valid.astype(f32).astype(bf16),
        jnp.where(spread, 1.0, 0.0).astype(bf16),
        preferred_element_type=f32,
    )
    part8 = lax.rem(lax.broadcasted_iota(jnp.int32, (8, 512), 1), 8)
    owned = [
        jnp.where(jnp.logical_and(wanted > 0.0, part8 == q), 1.0, 0.0) for q in range(4)
    ]
    asking = owned + [jnp.where(part8 >= 4, wanted, 0.0)]
    owned = jnp.concatenate(owned, axis=0)
    asking = jnp.concatenate(asking, axis=0)
    valid = jnp.concatenate([valid] * 4, axis=0)

    angles = long.astype(f32) * base_ref[...]
    cosine = jnp.cos(angles)
    sine = jnp.where(lane < 64, -jnp.sin(angles), jnp.sin(angles))

    own_pay.wait()
    own_w.wait()
    for_each(1, 8, lambda k: send_pay(k).wait_recv())
    for k in range(2):
        have_w(lax.rem(x + 3 + 2 * k, 4) * 2 + 1 - k)
        have_w(lax.rem(x + 2, 4) * 2 + k)
    have_w(x * 2 + 1 - c)
    sums = dot_tn(gathered[...].reshape(512, 128), weights[...].reshape(512, 384))
    partial[...] = sums.reshape(16, 8, 384).astype(bf16)
    own_part = pltpu.make_async_copy(partial.at[yc], parts.at[yc], own.at[1])
    own_part.start()
    for_each(1, 16, lambda k: send_part(k).start())
    lane32 = lax.broadcasted_iota(jnp.int32, (32, 128), 1)

    def limit_page(e, carry):
        tokens = jnp.sum(jnp.where(lane32 == e, valid, 0), axis=1, keepdims=True)
        limits[e] = jnp.where(lane32 < tokens, 0.0, NEG_FILL)
        return carry

    lax.fori_loop(0, 64, limit_page, 0, unroll=8)
    own_part.wait()
    for_each(1, 16, lambda k: send_part(k).wait_recv())
    total = parts[0:2].astype(f32)
    for i in range(1, 8):
        total = total + parts[2 * i : 2 * i + 2].astype(f32)
    made = [total[h // 3, :, 128 * (h % 3) : 128 * (h % 3) + 128] for h in range(6)]

    def turn(v):
        return (v * cosine + pltpu.roll(v, 64, 1) * sine).astype(bf16).astype(f32)

    queries = jnp.concatenate([turn(made[q]) for q in range(4)], axis=0)
    new_keys = jnp.concatenate([turn(made[4])] * 4, axis=0)
    new_values = jnp.concatenate([made[5].astype(bf16).astype(f32)] * 4, axis=0)
    self_scores = jnp.sum(queries * new_keys, axis=1, keepdims=True) * SCALE
    ask_rows = dot_tn(
        asking.astype(bf16),
        jnp.concatenate([queries, jnp.ones((8, 128), f32)], axis=0).astype(bf16),
    )
    ask_buf[...] = ask_rows.reshape(64, 8, 128).astype(bf16)
    own_ask = pltpu.make_async_copy(ask_buf.at[req], asked.at[req], own.at[1])
    own_ask.start()
    for_each(1, 64, lambda k: ask(k).start())
    load.wait()

    queries = queries.astype(bf16)

    def score(e, top):
        s = dot_nt(queries, pages[e, :, 0:128]) * SCALE
        s = jnp.where(limits[e] == 0.0, s, NEG_FILL)
        scores[e] = s
        return jnp.maximum(top, s)

    near_max = lax.fori_loop(0, 64, score, jnp.full((32, 128), NEG_FILL, f32), unroll=8)
    near_max = jnp.max(near_max, axis=1, keepdims=True)

    own_ask.wait()
    batch = 16
    row3 = lax.broadcasted_iota(jnp.int32, (batch, 8, 128), 1)
    lane3 = lax.broadcasted_iota(jnp.int32, (batch, 8, 128), 2)
    own_answer = pltpu.make_async_copy(reply.at[req], back.at[req], r5.at[0])

    def serve(j, carry):
        first = j * batch

        @pl.when(j > 0)
        def _():
            ask(first).wait_recv()

        for_each(1, batch, lambda i: ask(first + i).wait_recv())
        sources = [lax.rem(req - first - i + 64, 64) for i in range(batch)]
        slots = [slots_ref[g] for g in sources]
        query, limit = [], []
        for g in sources:
            both = asked[g].astype(f32)
            other = pltpu.roll(both, 4, 0)
            query.append(jnp.where(row < 4, both, other).astype(bf16))
            limit.append(jnp.where(row < 4, other, both))
        limit = jnp.stack(limit)
        s = jnp.stack([dot_nt(query[i], pages[slots[i], :, 0:128]) for i in range(batch)]) * SCALE
        mask = lane3.astype(f32) < limit
        s = jnp.where(mask, s, NEG_FILL)
        m = jnp.max(s, axis=2, keepdims=True)
        w = jnp.where(mask, jnp.exp(s - m), 0.0)
        l = jnp.sum(w, axis=2, keepdims=True)
        m0, m1, m2 = split_three(jnp.broadcast_to(m, s.shape))
        l0, l1, l2 = split_three(jnp.broadcast_to(l, s.shape))
        stats = jnp.where(lane3 < 16, m0, jnp.where(lane3 < 32, m1, jnp.where(lane3 < 48, m2,
                jnp.where(lane3 < 64, l0, jnp.where(lane3 < 80, l1, l2)))))
        for i in range(batch):
            a = jnp.dot(
                w[i].astype(bf16), pages[slots[i], :, 128:256], preferred_element_type=f32
            )
            reply[sources[i]] = jnp.where(row < 4, a, stats[i]).astype(bf16)
        @pl.when(j > 0)
        def _():
            answer(first).start()

        for_each(1, batch, lambda i: answer(first + i).start())
        return carry

    lax.fori_loop(0, 64 // batch, serve, 0)
    own_answer.start()
    for_each(1, 8, lambda k: send_wo(k).start())
    def gather(e, carry):
        acc, weight = carry
        s = scores[e]
        w = jnp.where(s > 0.5 * NEG_FILL, jnp.exp(s - near_max), 0.0)
        return acc + jnp.dot(w.astype(bf16), pages[e, :, 128:256], preferred_element_type=f32), weight + w

    zero = jnp.zeros((32, 128), f32)
    near, near_sum = lax.fori_loop(0, 64, gather, (zero, zero), unroll=8)
    near_sum = jnp.sum(near_sum, axis=1, keepdims=True)

    pltpu.make_async_copy(back, back, r5.at[0]).wait()

    far = back[...].astype(f32).reshape(512, 128).astype(bf16)
    pick_max = jnp.logical_and(lane < 48, lax.rem(lane, 16) == 0)
    pick_sum = jnp.logical_and(
        jnp.logical_and(lane >= 48, lane < 96), lax.rem(lane, 16) == 0
    )
    far_max = dot_nt(jnp.where(pick_max, 1.0, 0.0).astype(bf16), far)
    far_sum = dot_nt(jnp.where(pick_sum, 1.0, 0.0).astype(bf16), far)
    far_max = jnp.concatenate([pltpu.roll(far_max, 508, 1)] * 4, axis=0)
    far_sum = jnp.concatenate([pltpu.roll(far_sum, 508, 1)] * 4, axis=0)
    picked = owned > 0.5
    peak = jnp.max(jnp.where(picked, far_max, NEG_FILL), axis=1, keepdims=True)
    peak = jnp.maximum(jnp.maximum(peak, near_max), self_scores)
    factors = jnp.where(picked, jnp.exp(jnp.minimum(far_max - peak, 0.0)), 0.0)
    near_factor = jnp.exp(near_max - peak)
    self_factor = jnp.exp(self_scores - peak)
    weight_sum = (
        jnp.sum(jnp.where(picked, factors * far_sum, 0.0), axis=1, keepdims=True)
        + near_factor * near_sum + self_factor
    )
    high = factors.astype(bf16)
    low = (factors - high.astype(f32)).astype(bf16)
    weighted = (
        jnp.dot(high, far, preferred_element_type=f32)
        + jnp.dot(low, far, preferred_element_type=f32)
        + near_factor * near + self_factor * new_values
    )
    heads_buf[...] = (weighted / weight_sum).astype(bf16)

    own_rows = pltpu.make_async_copy(heads_buf, rows.at[y], own.at[0])
    own_rows.start()
    for_each(1, 8, lambda k: send_rows(k).start())
    own_wo.wait()
    for_each(1, 8, lambda k: send_wo(k).wait_recv())
    own_rows.wait()
    for_each(1, 8, lambda k: send_rows(k).wait_recv())
    heads = rows[...].astype(f32)
    heads = jnp.concatenate(
        [heads[:, 8 * q : 8 * q + 8].reshape(64, 128) for q in range(4)], axis=1
    ).astype(bf16)
    for i in range(8):
        tile = dot_nt(heads, wide[i])
        for k in range(2):
            piece[2 * i + k] = jnp.concatenate(
                [tile[32 * k : 32 * k + 16], tile[32 * k + 16 : 32 * k + 32]], axis=1
            ).astype(bf16)

    def send(k):
        @pl.when(is_me(dest(k)))
        def _():
            pltpu.make_async_copy(piece.at[k], pieces.at[spot], r7.at[spot]).start()

        @pl.when(jnp.logical_not(is_me(dest(k))))
        def _():
            push(k).start()

    for_each(0, 16, send)
    for_each(1, 64, lambda k: ask(k).wait_send())
    for_each(1, 64, lambda k: answer(k).wait_send())
    for_each(1, 8, lambda k: send_pay(k).wait_send())
    for_each(0, 4, lambda k: send_w(k).wait_send())
    near_w().wait_send()
    for k in range(2):
        pass_w(k).wait_send()
    for_each(1, 16, lambda k: send_part(k).wait_send())
    for_each(1, 8, lambda k: send_wo(k).wait_send())
    for_each(1, 8, lambda k: send_rows(k).wait_send())

    def receive(k):
        pltpu.make_async_copy(pieces.at[k], pieces.at[k], r7.at[k]).wait()

    for_each(0, 16, receive)
    totals = []
    for j in range(2):
        total = pieces[8 * j].astype(f32)
        for h in range(1, 8):
            total = total + pieces[8 * j + h].astype(f32)
        totals.append(jnp.concatenate([total[:, 0:64], total[:, 64:128]], axis=0))
    out_ref[...] = jnp.concatenate(
        [totals[j][8 * i : 8 * i + 8] for i in range(4) for j in range(2)], axis=0
    ).astype(bf16)

    def sent(k):
        @pl.when(jnp.logical_not(is_me(dest(k))))
        def _():
            push(k).wait_send()

    for_each(0, 16, sent)


def vmem():
    return pl.BlockSpec(memory_space=pltpu.VMEM)


def params(ident):
    return pltpu.CompilerParams(collective_id=ident, has_side_effects=True)


def dma(count):
    return pltpu.SemaphoreType.DMA((count,))


def shards(hidden, query_key_value_weight, output_weight, kv_pool, lengths, page_table, send_slots):
    bf16, f32 = jnp.bfloat16, jnp.float32
    exponent = np.arange(128) % 64 * (2.0 / 128)
    base = np.broadcast_to(ROPE_BASE ** -exponent, (8, 128)).astype(np.float32)
    smem = pl.BlockSpec(memory_space=pltpu.SMEM)
    return pl.pallas_call(
        layer_kernel,
        out_shape=jax.ShapeDtypeStruct((64, 64), bf16),
        in_specs=[smem, smem] + [vmem()] * 5 + [pl.BlockSpec(memory_space=pl.ANY)],
        out_specs=vmem(),
        scratch_shapes=[
            pltpu.VMEM((8, 64, 128), bf16),
            pltpu.VMEM((8, 64, 384), bf16),
            pltpu.VMEM((8, 64, 512), bf16),
            pltpu.VMEM((16, 8, 384), bf16),
            pltpu.VMEM((16, 8, 384), bf16),
            pltpu.VMEM((64, 128, 256), bf16),
            pltpu.VMEM((64, 32, 128), f32),
            pltpu.VMEM((64, 8, 128), bf16),
            pltpu.VMEM((64, 8, 128), bf16),
            pltpu.VMEM((64, 32, 128), f32),
            pltpu.VMEM((64, 8, 128), bf16),
            pltpu.VMEM((64, 8, 128), bf16),
            pltpu.VMEM((32, 128), bf16),
            pltpu.VMEM((8, 32, 128), bf16),
            pltpu.VMEM((16, 16, 128), bf16),
            pltpu.VMEM((16, 16, 128), bf16),
            dma(4), dma(8), dma(8), dma(16), dma(16), dma(8), dma(8), dma(64), dma(64),
            dma(64), dma(1), dma(8), dma(8), dma(16), dma(16),
            dma(7), dma(8),
        ],
        compiler_params=params(1),
    )(
        send_slots, lengths, page_table, jnp.asarray(base),
        hidden.T, query_key_value_weight.reshape(64, 768), output_weight.T, kv_pool.reshape(64, 128, 256),
    )


def solution(mesh):
    return jax.shard_map(
        shards,
        mesh=mesh,
        in_specs=(
            P(None, "req"),
            P("req", "head", None),
            P("head", "req"),
            P("req", "head", None, None),
            P("req"),
            P("req", None),
            P("req"),
        ),
        out_specs=P("head", "req"),
        check_vma=False,
    )
```

```python
import jax
import jax.numpy as jnp
import numpy as np
from jax import lax
from jax.experimental import pallas as pl
from jax.experimental.pallas import tpu as pltpu
from jax.sharding import PartitionSpec as P

ROPE_BASE = 500000.0
NEG_FILL = -1e30
SCALE = 128 ** (-0.5)


def remote(src, dst, send, recv, req, head=None):
    where = {"req": req} if head is None else {"req": req, "head": head}
    return pltpu.make_async_remote_copy(
        src_ref=src, dst_ref=dst, send_sem=send, recv_sem=recv,
        device_id=where, device_id_type=pl.DeviceIdType.MESH,
    )


def greet(barrier, req, head=None):
    where = {"req": req} if head is None else {"req": req, "head": head}
    pl.semaphore_signal(barrier, inc=1, device_id=where, device_id_type=pl.DeviceIdType.MESH)


def for_each(start, stop, body):
    def step(i, carry):
        body(i)
        return carry
    unroll = {63: 21, 15: 15, 16: 8, 7: 7, 4: 4}.get(stop - start, 1)
    lax.fori_loop(start, stop, step, 0, unroll=unroll)


def place(req):
    return req // 16, lax.rem(req // 2, 8), lax.rem(req, 2)


def split_three(v):
    high = v.astype(jnp.bfloat16).astype(jnp.float32)
    rest = v - high
    mid = rest.astype(jnp.bfloat16).astype(jnp.float32)
    return high, mid, rest - mid


def dot_nt(a, b):
    return lax.dot_general(a, b, (((1,), (1,)), ((), ())), preferred_element_type=jnp.float32)


def dot_tn(a, b):
    return lax.dot_general(a, b, (((0,), (0,)), ((), ())), preferred_element_type=jnp.float32)


def layer_kernel(
    slots_ref, lengths_ref, table_ref, base_ref, hid_ref, w_ref, wo_ref, kv_ref, out_ref,
    gathered, weights, wide, partial, parts, pages, limits, ask_buf, asked, scores, reply, back, heads_buf, rows,
    piece, pieces, own, s1, r1, s2, r2, s3, r3, s4, r4, s5, r5, s6, r6, s7, r7,
    s8, r8,
):
    bf16, f32 = jnp.bfloat16, jnp.float32
    req = lax.axis_index("req")
    z = lax.axis_index("head")
    x, y, c = place(req)
    xc = x * 2 + c
    yc = y * 2 + c
    mine = (z // 2) == x
    spot = c * 8 + z

    def at_xc(i):
        return (i // 2) * 16 + y * 2 + lax.rem(i, 2)

    def dest(k):
        return (k // 4) * 16 + y * 2 + lax.rem(k // 2, 2), x * 2 + lax.rem(k, 2)

    def origin(k):
        return (z // 2) * 16 + y * 2 + k // 8, lax.rem(k, 8)

    def is_me(pair):
        return jnp.logical_and(pair[0] == req, pair[1] == z)

    def block(i, width):
        return pl.ds(pl.multiple_of(i * width, width), width)

    barrier = pltpu.get_barrier_semaphore()
    for_each(1, 64, lambda k: greet(barrier, lax.rem(req + k, 64)))

    def hello(k):
        @pl.when(jnp.logical_not(is_me(origin(k))))
        def _():
            greet(barrier, *origin(k))

    for_each(0, 16, hello)
    load = pltpu.make_async_copy(kv_ref, pages, own.at[0])
    load.start()
    own_pay = pltpu.make_async_copy(hid_ref.at[:, block(x, 128)], gathered.at[xc], own.at[1])
    own_w = pltpu.make_async_copy(w_ref.at[:, block(c, 384)], weights.at[xc], own.at[3])
    own_wo = pltpu.make_async_copy(wo_ref, wide.at[xc], own.at[2])
    own_pay.start()
    own_w.start()
    own_wo.start()

    @pl.when(mine)
    def _():
        pl.semaphore_wait(barrier, 63 + 15)

    @pl.when(jnp.logical_not(mine))
    def _():
        pl.semaphore_wait(barrier, 63 + 16)

    def send_pay(k):
        peer = lax.rem(xc + k, 8)
        return remote(
            hid_ref.at[:, block(peer // 2, 128)], gathered.at[xc], s1.at[k], r1.at[k], at_xc(peer)
        )

    def send_w(k):
        far = lax.rem(x + 1 + 2 * (k // 2), 4) * 2 + lax.rem(k, 2)
        return remote(
            w_ref.at[:, block(lax.rem(k, 2), 384)], weights.at[xc], s8.at[k], r8.at[xc], at_xc(far)
        )

    def near_w():
        return remote(
            w_ref.at[:, block(1 - c, 384)], weights.at[xc], s8.at[4], r8.at[xc],
            at_xc(x * 2 + 1 - c),
        )

    def pass_w(k):
        source = lax.rem(x + 3 + 2 * k, 4) * 2 + k
        target = lax.rem(x + 1 + 2 * k, 4) * 2 + c
        return remote(
            weights.at[source], weights.at[source], s8.at[5 + k], r8.at[source], at_xc(target)
        )

    def have_w(source):
        remote(
            weights.at[source], weights.at[source], s8.at[0], r8.at[source], at_xc(source)
        ).wait_recv()

    def send_part(k):
        peer = lax.rem(yc + k, 16)
        return remote(partial.at[peer], parts.at[yc], s2.at[k], r2.at[k], x * 16 + peer)

    def send_wo(k):
        peer = lax.rem(xc + k, 8)
        return remote(wo_ref, wide.at[xc], s3.at[k], r3.at[k], at_xc(peer))

    def ask(k):
        peer = lax.rem(req + k, 64)
        return remote(ask_buf.at[peer], asked.at[req], s4.at[0], r4.at[k // 16], peer)

    def answer(k):
        peer = lax.rem(req - k + 64, 64)
        return remote(reply.at[peer], back.at[req], s5.at[0], r5.at[0], peer)

    def send_rows(k):
        peer = x * 16 + lax.rem(y + k, 8) * 2 + c
        return remote(heads_buf, rows.at[y], s6.at[k], r6.at[k], peer)

    def push(k):
        return remote(piece.at[k], pieces.at[spot], s7.at[k], r7.at[spot], *dest(k))

    for_each(0, 4, lambda k: send_w(k).start())
    for_each(1, 8, lambda k: send_pay(k).start())
    near_w().start()
    for k in range(2):
        have_w(lax.rem(x + 3 + 2 * k, 4) * 2 + k)
        pass_w(k).start()

    row = lax.broadcasted_iota(jnp.int32, (8, 128), 0)
    lane = lax.broadcasted_iota(jnp.int32, (8, 128), 1)
    long = jnp.zeros((8, 128), jnp.int32)
    for i in range(8):
        long = jnp.where(row == i, lengths_ref[i], long)
    table = table_ref[...]
    valid = jnp.zeros((8, 128), jnp.int32)
    for p in range(16):
        tokens = jnp.clip(long - p * 128, 0, 128)
        valid = valid + jnp.where(table[:, p : p + 1] == lane, tokens, 0)
    spread = (
        lax.broadcasted_iota(jnp.int32, (128, 512), 0) - 64
        == lax.broadcasted_iota(jnp.int32, (128, 512), 1) // 8
    )
    wanted = jnp.dot(
        valid.astype(f32).astype(bf16),
        jnp.where(spread, 1.0, 0.0).astype(bf16),
        preferred_element_type=f32,
    )
    part8 = lax.rem(lax.broadcasted_iota(jnp.int32, (8, 512), 1), 8)
    owned = [
        jnp.where(jnp.logical_and(wanted > 0.0, part8 == q), 1.0, 0.0) for q in range(4)
    ]
    asking = owned + [jnp.where(part8 >= 4, wanted, 0.0)]
    owned = jnp.concatenate(owned, axis=0)
    asking = jnp.concatenate(asking, axis=0)
    valid = jnp.concatenate([valid] * 4, axis=0)

    angles = long.astype(f32) * base_ref[...]
    cosine = jnp.cos(angles)
    sine = jnp.where(lane < 64, -jnp.sin(angles), jnp.sin(angles))

    own_pay.wait()
    own_w.wait()
    for_each(1, 8, lambda k: send_pay(k).wait_recv())
    for k in range(2):
        have_w(lax.rem(x + 3 + 2 * k, 4) * 2 + 1 - k)
        have_w(lax.rem(x + 2, 4) * 2 + k)
    have_w(x * 2 + 1 - c)
    sums = dot_tn(gathered[...].reshape(512, 128), weights[...].reshape(512, 384))
    partial[...] = sums.reshape(16, 8, 384).astype(bf16)
    own_part = pltpu.make_async_copy(partial.at[yc], parts.at[yc], own.at[1])
    own_part.start()
    for_each(1, 16, lambda k: send_part(k).start())
    lane32 = lax.broadcasted_iota(jnp.int32, (32, 128), 1)

    def limit_page(e, carry):
        tokens = jnp.sum(jnp.where(lane32 == e, valid, 0), axis=1, keepdims=True)
        limits[e] = jnp.where(lane32 < tokens, 0.0, NEG_FILL)
        return carry

    lax.fori_loop(0, 64, limit_page, 0, unroll=8)
    own_part.wait()
    for_each(1, 16, lambda k: send_part(k).wait_recv())
    total = parts[0:2].astype(f32)
    for i in range(1, 8):
        total = total + parts[2 * i : 2 * i + 2].astype(f32)
    made = [total[h // 3, :, 128 * (h % 3) : 128 * (h % 3) + 128] for h in range(6)]

    def turn(v):
        return (v * cosine + pltpu.roll(v, 64, 1) * sine).astype(bf16).astype(f32)

    queries = jnp.concatenate([turn(made[q]) for q in range(4)], axis=0)
    new_keys = jnp.concatenate([turn(made[4])] * 4, axis=0)
    new_values = jnp.concatenate([made[5].astype(bf16).astype(f32)] * 4, axis=0)
    self_scores = jnp.sum(queries * new_keys, axis=1, keepdims=True) * SCALE
    ask_rows = dot_tn(
        asking.astype(bf16),
        jnp.concatenate([queries, jnp.ones((8, 128), f32)], axis=0).astype(bf16),
    )
    ask_buf[...] = ask_rows.reshape(64, 8, 128).astype(bf16)
    own_ask = pltpu.make_async_copy(ask_buf.at[req], asked.at[req], r4.at[0])
    own_ask.start()
    for_each(1, 64, lambda k: ask(k).start())
    load.wait()

    queries = queries.astype(bf16)

    def score(e, top):
        s = dot_nt(queries, pages[e, :, 0:128]) * SCALE
        s = jnp.where(limits[e] == 0.0, s, NEG_FILL)
        scores[e] = s
        return jnp.maximum(top, s)

    near_max = lax.fori_loop(0, 64, score, jnp.full((32, 128), NEG_FILL, f32), unroll=8)
    near_max = jnp.max(near_max, axis=1, keepdims=True)

    batch = 16
    row3 = lax.broadcasted_iota(jnp.int32, (batch, 8, 128), 1)
    lane3 = lax.broadcasted_iota(jnp.int32, (batch, 8, 128), 2)
    own_answer = pltpu.make_async_copy(reply.at[req], back.at[req], r5.at[0])

    def serve(j, carry):
        first = j * batch

        filled = asked.at[pl.ds(0, batch)]
        pltpu.make_async_copy(filled, filled, r4.at[j]).wait()
        sources = [lax.rem(req - first - i + 64, 64) for i in range(batch)]
        slots = [slots_ref[g] for g in sources]
        query, limit = [], []
        for g in sources:
            both = asked[g].astype(f32)
            other = pltpu.roll(both, 4, 0)
            query.append(jnp.where(row < 4, both, other).astype(bf16))
            limit.append(jnp.where(row < 4, other, both))
        limit = jnp.stack(limit)
        s = jnp.stack([dot_nt(query[i], pages[slots[i], :, 0:128]) for i in range(batch)]) * SCALE
        mask = lane3.astype(f32) < limit
        s = jnp.where(mask, s, NEG_FILL)
        m = jnp.max(s, axis=2, keepdims=True)
        w = jnp.where(mask, jnp.exp(s - m), 0.0)
        l = jnp.sum(w, axis=2, keepdims=True)
        m0, m1, m2 = split_three(jnp.broadcast_to(m, s.shape))
        l0, l1, l2 = split_three(jnp.broadcast_to(l, s.shape))
        stats = jnp.where(lane3 < 16, m0, jnp.where(lane3 < 32, m1, jnp.where(lane3 < 48, m2,
                jnp.where(lane3 < 64, l0, jnp.where(lane3 < 80, l1, l2)))))
        for i in range(batch):
            a = jnp.dot(
                w[i].astype(bf16), pages[slots[i], :, 128:256], preferred_element_type=f32
            )
            reply[sources[i]] = jnp.where(row < 4, a, stats[i]).astype(bf16)
        @pl.when(j > 0)
        def _():
            answer(first).start()

        for_each(1, batch, lambda i: answer(first + i).start())
        return carry

    lax.fori_loop(0, 64 // batch, serve, 0)
    own_answer.start()
    for_each(1, 8, lambda k: send_wo(k).start())
    def gather(e, carry):
        acc, weight = carry
        s = scores[e]
        w = jnp.where(s > 0.5 * NEG_FILL, jnp.exp(s - near_max), 0.0)
        return acc + jnp.dot(w.astype(bf16), pages[e, :, 128:256], preferred_element_type=f32), weight + w

    zero = jnp.zeros((32, 128), f32)
    near, near_sum = lax.fori_loop(0, 64, gather, (zero, zero), unroll=8)
    near_sum = jnp.sum(near_sum, axis=1, keepdims=True)

    pltpu.make_async_copy(back, back, r5.at[0]).wait()

    far = back[...].astype(f32).reshape(512, 128).astype(bf16)
    pick_max = jnp.logical_and(lane < 48, lax.rem(lane, 16) == 0)
    pick_sum = jnp.logical_and(
        jnp.logical_and(lane >= 48, lane < 96), lax.rem(lane, 16) == 0
    )
    far_max = dot_nt(jnp.where(pick_max, 1.0, 0.0).astype(bf16), far)
    far_sum = dot_nt(jnp.where(pick_sum, 1.0, 0.0).astype(bf16), far)
    far_max = jnp.concatenate([pltpu.roll(far_max, 508, 1)] * 4, axis=0)
    far_sum = jnp.concatenate([pltpu.roll(far_sum, 508, 1)] * 4, axis=0)
    picked = owned > 0.5
    peak = jnp.max(jnp.where(picked, far_max, NEG_FILL), axis=1, keepdims=True)
    peak = jnp.maximum(jnp.maximum(peak, near_max), self_scores)
    factors = jnp.where(picked, jnp.exp(jnp.minimum(far_max - peak, 0.0)), 0.0)
    near_factor = jnp.exp(near_max - peak)
    self_factor = jnp.exp(self_scores - peak)
    weight_sum = (
        jnp.sum(jnp.where(picked, factors * far_sum, 0.0), axis=1, keepdims=True)
        + near_factor * near_sum + self_factor
    )
    high = factors.astype(bf16)
    low = (factors - high.astype(f32)).astype(bf16)
    weighted = (
        jnp.dot(high, far, preferred_element_type=f32)
        + jnp.dot(low, far, preferred_element_type=f32)
        + near_factor * near + self_factor * new_values
    )
    heads_buf[...] = (weighted / weight_sum).astype(bf16)

    own_rows = pltpu.make_async_copy(heads_buf, rows.at[y], own.at[0])
    own_rows.start()
    for_each(1, 8, lambda k: send_rows(k).start())
    own_wo.wait()
    for_each(1, 8, lambda k: send_wo(k).wait_recv())
    own_rows.wait()
    for_each(1, 8, lambda k: send_rows(k).wait_recv())
    heads = rows[...].astype(f32)
    heads = jnp.concatenate(
        [heads[:, 8 * q : 8 * q + 8].reshape(64, 128) for q in range(4)], axis=1
    ).astype(bf16)
    for i in range(8):
        tile = dot_nt(heads, wide[i])
        for k in range(2):
            piece[2 * i + k] = jnp.concatenate(
                [tile[32 * k : 32 * k + 16], tile[32 * k + 16 : 32 * k + 32]], axis=1
            ).astype(bf16)

    def send(k):
        @pl.when(is_me(dest(k)))
        def _():
            pltpu.make_async_copy(piece.at[k], pieces.at[spot], r7.at[spot]).start()

        @pl.when(jnp.logical_not(is_me(dest(k))))
        def _():
            push(k).start()

    for_each(0, 16, send)
    for buffer, sem in ((ask_buf, s4.at[0]), (reply, s5.at[0])):
        left = buffer.at[pl.ds(0, 63)]
        pltpu.make_async_copy(left, left, sem).wait()
    for_each(1, 8, lambda k: send_pay(k).wait_send())
    for_each(0, 4, lambda k: send_w(k).wait_send())
    near_w().wait_send()
    for k in range(2):
        pass_w(k).wait_send()
    for_each(1, 16, lambda k: send_part(k).wait_send())
    for_each(1, 8, lambda k: send_wo(k).wait_send())
    for_each(1, 8, lambda k: send_rows(k).wait_send())

    def receive(k):
        pltpu.make_async_copy(pieces.at[k], pieces.at[k], r7.at[k]).wait()

    for_each(0, 16, receive)
    totals = []
    for j in range(2):
        total = pieces[8 * j].astype(f32)
        for h in range(1, 8):
            total = total + pieces[8 * j + h].astype(f32)
        totals.append(jnp.concatenate([total[:, 0:64], total[:, 64:128]], axis=0))
    out_ref[...] = jnp.concatenate(
        [totals[j][8 * i : 8 * i + 8] for i in range(4) for j in range(2)], axis=0
    ).astype(bf16)

    def sent(k):
        @pl.when(jnp.logical_not(is_me(dest(k))))
        def _():
            push(k).wait_send()

    for_each(0, 16, sent)


def vmem():
    return pl.BlockSpec(memory_space=pltpu.VMEM)


def params(ident):
    return pltpu.CompilerParams(collective_id=ident, has_side_effects=True)


def dma(count):
    return pltpu.SemaphoreType.DMA((count,))


def shards(hidden, query_key_value_weight, output_weight, kv_pool, lengths, page_table, send_slots):
    bf16, f32 = jnp.bfloat16, jnp.float32
    exponent = np.arange(128) % 64 * (2.0 / 128)
    base = np.broadcast_to(ROPE_BASE ** -exponent, (8, 128)).astype(np.float32)
    smem = pl.BlockSpec(memory_space=pltpu.SMEM)
    return pl.pallas_call(
        layer_kernel,
        out_shape=jax.ShapeDtypeStruct((64, 64), bf16),
        in_specs=[smem, smem] + [vmem()] * 5 + [pl.BlockSpec(memory_space=pl.ANY)],
        out_specs=vmem(),
        scratch_shapes=[
            pltpu.VMEM((8, 64, 128), bf16),
            pltpu.VMEM((8, 64, 384), bf16),
            pltpu.VMEM((8, 64, 512), bf16),
            pltpu.VMEM((16, 8, 384), bf16),
            pltpu.VMEM((16, 8, 384), bf16),
            pltpu.VMEM((64, 128, 256), bf16),
            pltpu.VMEM((64, 32, 128), f32),
            pltpu.VMEM((64, 8, 128), bf16),
            pltpu.VMEM((64, 8, 128), bf16),
            pltpu.VMEM((64, 32, 128), f32),
            pltpu.VMEM((64, 8, 128), bf16),
            pltpu.VMEM((64, 8, 128), bf16),
            pltpu.VMEM((32, 128), bf16),
            pltpu.VMEM((8, 32, 128), bf16),
            pltpu.VMEM((16, 16, 128), bf16),
            pltpu.VMEM((16, 16, 128), bf16),
            dma(4), dma(8), dma(8), dma(16), dma(16), dma(8), dma(8), dma(1), dma(4),
            dma(1), dma(1), dma(8), dma(8), dma(16), dma(16),
            dma(7), dma(8),
        ],
        compiler_params=params(1),
    )(
        send_slots, lengths, page_table, jnp.asarray(base),
        hidden.T, query_key_value_weight.reshape(64, 768), output_weight.T, kv_pool.reshape(64, 128, 256),
    )


def solution(mesh):
    return jax.shard_map(
        shards,
        mesh=mesh,
        in_specs=(
            P(None, "req"),
            P("req", "head", None),
            P("head", "req"),
            P("req", "head", None, None),
            P("req"),
            P("req", None),
            P("req"),
        ),
        out_specs=P("head", "req"),
        check_vma=False,
    )
```
